256 devices in a mesh: sub: 4 (over z_lo), coarse: 64 (over x, z_hi, y, core).
Axes of the slice: x: 4, y: 4, z: 8 (z_hi: 2, z_lo: 4; z = z_hi * 4 + z_lo), core: 2. Of those that a mesh axis runs over, the one named last changes fastest.
Arguments:
- schur_inverse: bfloat16 [512, 1536, 1536], P(('sub', 'coarse')), may hold values from -1 to 2, as said below
- corner_coupling: bfloat16 [512, 24, 1536], P(('sub', 'coarse')), may hold values from -0.21875 to 0.21875
- coarse_inverse: bfloat16 [4, 64, 24, 6144], P(None, 'coarse', None, 'sub'), may hold values from -1 to 2, as said below
- load_cases: bfloat16 [512, 16, 1536], P(('sub', 'coarse')), may hold values from -16 to 16
- face_order: int32 [512, 768], P(('sub', 'coarse')), may hold values from 0 to 767, each once within a row
- corner_dofs: int32 [512, 24], P(('sub', 'coarse')), may hold values from 0 to 6143, as said below
- scene_loads: int32 [128, 2], replicated, may hold values from 0 to 15
- scene_weights: float32 [128, 2], replicated, may hold values from 0.3 to 3
Outputs:
- multipliers: float32 [512, 128, 768], P(('sub', 'coarse'))
- residual: float32 [512, 128, 768], P(('sub', 'coarse'))
The draws below stay inside these ranges and needn't reach their ends.
Inputs may be any that keep to these rules, and one draw needn't show every extreme that they name: `schur_inverse`: each subdomain's block is symmetric positive definite. `coarse_inverse`: K as defined in the reference program is symmetric positive definite. `corner_dofs`: every entry of row n has the form (a * 64 + c) * 24 + r with c the group of subdomain n, 0 <= a < 4 and 0 <= r < 24; every coarse dof of a group is named by exactly 2 entries of that group's rows.
All inputs are finite; a program needn't handle non-finite values.
Results may differ from the reference program's by a relative error of at most 0.034.
Values may be sent and summed in bfloat16 or wider, within the bound.
A program may use at most 64 MiB of HBM per device.

```python
import math
import jax
import jax.numpy as jnp
from jax import lax

FACE = 768
CORNERS = 24
LOADS = 16
ITERS = 2
SCENES = 128
SUB_DEV = 2
IFACE = 1536
NSUBS = 512
COARSE = 6144
N_SUB = 4
N_COARSE = 64


def dominant_block(key, matrix_order):
    noise_key, diag_key = jax.random.split(key)
    noise_part = jax.random.normal(noise_key, (matrix_order, matrix_order), jnp.float32)
    diagonal = jax.random.uniform(diag_key, (matrix_order,), jnp.float32, 0.8, 1.6)
    symmetric = (noise_part + noise_part.T) * (0.25 / math.sqrt(2.0 * matrix_order))
    return symmetric + jnp.diag(diagonal)


def draw_schur_inverse(key, part):
    all_keys = jax.random.split(jax.random.fold_in(key, 3), NSUBS)
    return lax.map(lambda sub_key: dominant_block(sub_key, IFACE).astype(jnp.bfloat16), all_keys)


def draw_coarse_inverse(key, part):
    matrix = dominant_block(jax.random.fold_in(key, 5), COARSE).astype(jnp.bfloat16)
    return matrix.reshape(N_SUB, N_COARSE, CORNERS, COARSE)


def draw_load_cases(key, part):
    base_key, jitter_key = jax.random.split(jax.random.fold_in(key, 7))
    position = jnp.arange(NSUBS, dtype=jnp.float32) / max(NSUBS - 1, 1)
    jitter = jnp.exp(jax.random.uniform(jitter_key, (NSUBS,), jnp.float32, -0.35, 0.35))
    base_values = jnp.clip(jax.random.normal(base_key, (NSUBS, LOADS, IFACE), jnp.float32), -6.0, 6.0)
    rising = jnp.exp(math.log(3.0) * position) * jitter
    return (base_values * rising[:, None, None] * 0.6).astype(jnp.bfloat16)


def draw_corner_dofs(key, part):
    span_size = N_SUB * CORNERS
    all_keys = jax.random.split(jax.random.fold_in(key, 11), N_COARSE * SUB_DEV)
    shuffled = jax.vmap(lambda one_key: jax.random.permutation(one_key, span_size))(all_keys)
    local_dofs = shuffled.reshape(N_COARSE, N_SUB * SUB_DEV, CORNERS)
    column_ids = jnp.arange(N_COARSE)[:, None, None]
    coarse_dof = (local_dofs // CORNERS * N_COARSE + column_ids) * CORNERS + local_dofs % CORNERS
    grouped = coarse_dof.reshape(N_COARSE, N_SUB, SUB_DEV, CORNERS)
    return jnp.swapaxes(grouped, 0, 1).reshape(N_SUB * N_COARSE * SUB_DEV, CORNERS).astype(jnp.int32)


def set_ends(entries, rng, smallest, top_value):
    spot = [jax.random.randint(jax.random.fold_in(rng, axis), (), 0, length) for axis, length in enumerate(entries.shape)]
    widest = entries.shape.index(max(entries.shape))
    next_to = spot[:widest] + [(spot[widest] + 1) % entries.shape[widest]] + spot[widest + 1:]
    return entries.at[tuple(spot)].set(smallest).at[tuple(next_to)].set(top_value)


def block_scale(rng, shape, cuts, least, high):
    def one(dim, blocks):
        heights = jax.random.uniform(jax.random.fold_in(jax.random.fold_in(rng, 6), dim), (blocks,), jnp.float32, least / len(cuts), high / len(cuts))
        return jnp.repeat(jnp.exp(heights), shape[dim] // blocks).reshape((-1,) + (1,) * (len(shape) - dim - 1))

    gain = one(*cuts[0])
    for cut in cuts[1:]:
        gain = gain * one(*cut)
    return gain


def bell_draw(rng, shape, width, limit, cuts=(), kind=jnp.bfloat16):
    entries = width * jax.random.normal(rng, shape, jnp.float32)
    if cuts:
        entries = entries * block_scale(rng, shape, cuts, -0.22, 0.18)
    return jnp.clip(entries, -limit, limit).astype(kind)


def setup_inputs(seed: int = 0) -> dict:
    seeds = jax.random.split(jax.random.key(seed), 9)
    return {
        "schur_inverse": draw_schur_inverse(jax.random.fold_in(seeds[8], 71), 0),
        "corner_coupling": bell_draw(seeds[1], (NSUBS, CORNERS, IFACE), (IFACE // 2) ** -0.5, 0.21875, ((0, 256),)),
        "coarse_inverse": draw_coarse_inverse(jax.random.fold_in(seeds[8], 71), 0),
        "load_cases": draw_load_cases(jax.random.fold_in(seeds[8], 71), 0),
        "face_order": jax.vmap(lambda own: jax.random.permutation(own, FACE))(jax.random.split(seeds[4], NSUBS)).reshape((NSUBS, FACE)).astype(jnp.int32),
        "corner_dofs": draw_corner_dofs(jax.random.fold_in(seeds[8], 71), 0),
        "scene_loads": set_ends(jax.random.randint(seeds[6], (SCENES, 2), 0, LOADS), jax.random.fold_in(seeds[6], 1), 0, LOADS - 1).astype(jnp.int32),
        "scene_weights": jnp.clip(jnp.exp(jax.random.uniform(seeds[7], (SCENES, 2), jnp.float32, math.log(0.3), math.log(3.0))), 0.3, 3.0),
    }


def chain_order(values):
    tail_shape = values.shape[1:]
    grouped = values.reshape((N_SUB, N_COARSE, SUB_DEV) + tail_shape)
    return jnp.swapaxes(grouped, 0, 1).reshape((N_COARSE, N_SUB * SUB_DEV) + tail_shape)


def block_order(values):
    tail_shape = values.shape[2:]
    grouped = values.reshape((N_COARSE, N_SUB, SUB_DEV) + tail_shape)
    return jnp.swapaxes(grouped, 0, 1).reshape((N_SUB * N_COARSE * SUB_DEV,) + tail_shape)


def permute_faces(values, indices):
    return jax.vmap(lambda one_block, one_order: jnp.take(one_block, one_order, axis=1))(values, indices)


def inverse_order(face_order):
    row_ids = jnp.arange(face_order.shape[0], dtype=jnp.int32)[:, None]
    ranked = jnp.broadcast_to(jnp.arange(face_order.shape[1], dtype=jnp.int32)[None, :], face_order.shape)
    return jnp.zeros_like(face_order).at[row_ids, face_order].set(ranked)


def reference(schur_inverse, corner_coupling, coarse_inverse, load_cases, face_order, corner_dofs, scene_loads, scene_weights):
    inverse_face = inverse_order(face_order)
    position = jnp.arange(N_SUB * SUB_DEV)
    heads = block_order(jnp.broadcast_to(position[None, :] == 0, (N_COARSE, N_SUB * SUB_DEV)))
    kernel = coarse_inverse.reshape(COARSE, COARSE)

    def transposed_jump(values):
        moved = chain_order(permute_faces(values, inverse_face))
        shifted = jnp.concatenate([moved[:, 1:], jnp.zeros_like(moved[:, :1])], axis=1)
        return jnp.concatenate([-values, block_order(shifted)], axis=2)

    def jump(displaced):
        right_faces = chain_order(displaced[:, :, FACE:])
        previous = jnp.concatenate([jnp.zeros_like(right_faces[:, :1]), right_faces[:, :-1]], axis=1)
        raw_jump = permute_faces(block_order(previous), face_order) - displaced[:, :, :FACE]
        return jnp.where(heads[:, None, None], 0.0, raw_jump)

    def primal_solve(loads):
        corner_terms = lax.map(lambda operands: jnp.dot(operands[0], operands[1].T, preferred_element_type=jnp.float32), (corner_coupling, loads))
        assembled = jnp.zeros((COARSE, SCENES), jnp.float32).at[corner_dofs.reshape(-1)].add(corner_terms.reshape(-1, SCENES))
        coarse_values = jnp.dot(kernel, assembled.astype(jnp.bfloat16), preferred_element_type=jnp.float32).astype(jnp.bfloat16)
        corner_values = coarse_values[corner_dofs]

        def one_subdomain(operands):
            local_part = jnp.dot(operands[0], operands[1], preferred_element_type=jnp.float32)
            return local_part + jnp.dot(operands[2].T, operands[3], preferred_element_type=jnp.float32)

        return lax.map(one_subdomain, (loads, schur_inverse, corner_values, corner_coupling))

    selection = (scene_loads[:, :, None] == jnp.arange(LOADS, dtype=jnp.int32)[None, None, :]).astype(jnp.float32)
    mixing = jnp.sum(selection * scene_weights[:, :, None], axis=1)
    external = jnp.einsum("sl,nlb->nsb", mixing, load_cases.astype(jnp.float32), precision=lax.Precision.HIGHEST).astype(jnp.bfloat16)

    residual = jump(primal_solve(external))
    direction = residual
    multipliers = jnp.zeros_like(residual)
    norm_now = jnp.sum(residual * residual, axis=(0, 2))
    for iteration in range(ITERS):
        image_dir = jump(primal_solve(transposed_jump(direction.astype(jnp.bfloat16))))
        step_size = norm_now / jnp.sum(direction * image_dir, axis=(0, 2))
        multipliers = multipliers + step_size[None, :, None] * direction
        residual = residual - step_size[None, :, None] * image_dir
        norm_next = jnp.sum(residual * residual, axis=(0, 2))
        direction = residual + (norm_next / norm_now)[None, :, None] * direction
        norm_now = norm_next
    return multipliers, residual
```

```python
import functools

import jax
import jax.numpy as jnp
from jax import lax
from jax.experimental import pallas as pl
from jax.experimental.pallas import tpu as pltpu
from jax.sharding import Mesh
from jax.sharding import PartitionSpec as P

AXES = ("sub", "coarse_0", "coarse_1", "coarse_2", "coarse_3")
COARSE = AXES[1:]
LANES = 128
SOLVES = 3
F32 = jnp.float32
BF16 = jnp.bfloat16


def contract(a, b, da, db):
    return lax.dot_general(a, b, (((da,), (db,)), ((), ())), preferred_element_type=F32)


def mm(a, b):
    return contract(a, b, 1, 0)


def upper_lower(a):
    upper = a.astype(BF16)
    return upper, (a - upper.astype(F32)).astype(BF16)


def kernel(
    sizes,
    schur,
    coupling,
    coarse,
    cases,
    order,
    dofs,
    scene_loads,
    scene_weights,
    x_out,
    r_out,
    S,
    fwd,
    bwd,
    K,
    Kt,
    D,
    Dt,
    E,
    Et,
    entry,
    f,
    base,
    left,
    W,
    Wn,
    cv,
    T,
    R,
    G,
    V,
    face_send,
    face_recv,
    right_send,
    right_recv,
    prev_coupling,
    own_entry,
    prev_entry,
    dots,
    dots_a,
    dots_b,
    coef,
    load_sem,
    send_sem,
    recv_sem,
    last_send,
    last_recv,
):
    n_sub, nx, nh, ny, nk = sizes
    nz = nh * n_sub
    corners = dofs.shape[1]
    face = order.shape[1]
    column = n_sub * corners
    s, x, h, y, k = (lax.axis_index(a) for a in AXES)
    z = h * n_sub + s
    xy = x * ny + y
    group = ((x * nh + h) * ny + y) * nk + k

    def at(sub=None, cx=None, ch=None, cy=None, ck=None):
        return (
            s if sub is None else sub,
            x if cx is None else cx,
            h if ch is None else ch,
            y if cy is None else cy,
            k if ck is None else ck,
        )

    def z_at(dz, dk=0):
        other = lax.rem(z + dz, nz)
        return at(sub=lax.rem(other, n_sub), ch=other // n_sub, ck=lax.rem(k + dk, nk))

    def xy_at(dx, dy):
        return at(cx=lax.rem(x + dx, nx), cy=lax.rem(y + dy, ny))

    z_steps = [(dz, dk) for dk in range(nk) for dz in range(nz) if (dz, dk) != (0, 0)]
    xy_steps = [(dx, dy) for dx in range(nx) for dy in range(ny) if (dx, dy) != (0, 0)]
    xy_steps.sort(key=lambda d: -(min(d[0], nx - d[0]) + min(d[1], ny - d[1])))
    greeted = [z_at(*d) for d in z_steps] + [xy_at(*d) for d in xy_steps]

    barrier = pltpu.get_barrier_semaphore()
    for device in greeted:
        pl.semaphore_signal(barrier, inc=1, device_id=device, device_id_type=pl.DeviceIdType.MESH)
    loads = [pltpu.make_async_copy(schur.at[j], S.at[j], load_sem.at[j]) for j in range(2)]
    for load in loads:
        load.start()

    sent = []

    def remote(src, dst, send, recv, device):
        return pltpu.make_async_remote_copy(
            src_ref=src,
            dst_ref=dst,
            send_sem=send,
            recv_sem=recv,
            device_id=device,
            device_id_type=pl.DeviceIdType.MESH,
        )

    SEM_XY = nz
    SEM_K = SEM_XY + nx * ny
    SEM_E = SEM_K + nx
    SEM_FACE = SEM_E + n_sub
    SEM_RIGHT = SEM_FACE + 1
    SEM_INIT = SEM_RIGHT + 1

    def copy(slot, number, src, dst, device):
        return remote(src, dst, send_sem.at[slot, number], recv_sem.at[slot, number], device)

    def start(c):
        c.start()
        sent.append(c)
        return c

    def iota(shape, dim):
        return lax.broadcasted_iota(jnp.int32, shape, dim)

    lane = iota((scene_loads.shape[0], LANES), 1)
    mixing = jnp.where(lane == scene_loads[:, 0:1], scene_weights[:, 0:1], 0.0)
    mixing = mixing + jnp.where(lane == scene_loads[:, 1:2], scene_weights[:, 1:2], 0.0)
    mixing = mixing.T[: cases.shape[1]]
    mix_0, rest = upper_lower(mixing)
    rest = mixing - mix_0.astype(F32)
    mix_1, mix_2 = upper_lower(rest)
    mix = jnp.concatenate([mix_0, mix_1, mix_2], axis=0)
    for j in range(2):
        thrice = jnp.concatenate([cases[j]] * 3, axis=0)
        f[j] = contract(thrice, mix, 0, 0).astype(BF16)

    eye = (iota((corners, corners), 0) == iota((corners, corners), 1)).astype(BF16)
    entry[...] = jnp.zeros_like(entry)
    total = jnp.zeros((LANES, LANES), F32)
    stride = nx * nh * ny * nk * corners
    for j in range(2):
        shifted = dofs[j : j + 1, :] - group * corners
        local = shifted
        for a in range(1, n_sub):
            local = local - jnp.where(shifted >= a * stride, stride - corners, 0)
        table = (iota((LANES, corners), 0) == local).astype(F32).astype(BF16)
        rows = contract(eye, table, 1, 1)
        if j == 0:
            entry[corners : 2 * corners, :] = rows
            entry[2 * corners : 3 * corners, :] = rows
        else:
            entry[3 * corners : 4 * corners, :] = rows
            own_entry[...] = rows.astype(BF16)
        for part in upper_lower(mm(coupling[j], f[j])):
            total = total + mm(table, part)

    pl.semaphore_wait(barrier, len(greeted))

    def send_column(slot, total):
        for a in range(n_sub):
            T[slot, a] = total[a * corners : (a + 1) * corners].astype(BF16)
        copies = [
            start(copy(slot, dz, T.at[slot, lax.rem(z + dz, n_sub)], R.at[slot, z], z_at(dz)))
            for dz in range(1, nz)
        ]
        R[slot, z] = T[slot, s]
        return copies

    copies_b = send_column(0, total)

    coupling_copy = copy(
        0, SEM_INIT, coupling.at[1, :, face:], prev_coupling, at(sub=lax.rem(s + 1, n_sub))
    )
    entry_copy = copy(0, SEM_INIT + 1, own_entry, prev_entry, at(sub=lax.rem(s + 1, n_sub)))

    @pl.when(s < n_sub - 1)
    def _():
        entry_copy.start()
        coupling_copy.start()

    def build_permutations(j):
        row = order[j : j + 1, :]
        for b in range(0, face, LANES):
            ids = iota((LANES, face), 0) + b
            bwd[j, b : b + LANES, :] = (ids == row).astype(F32).astype(BF16)
        spread = jnp.broadcast_to(row.astype(F32), (LANES, face)).T
        for b in range(0, face, LANES):
            ids = (iota((face, LANES), 1) + b).astype(F32)
            fwd[j, :, b : b + LANES] = (spread == ids).astype(F32).astype(BF16)

    def build_coarse():
        wide = coarse[...].astype(F32)
        if column < LANES:
            wide = jnp.concatenate([wide, jnp.zeros((LANES - column, wide.shape[1]), F32)], axis=0)
        turned = wide.T
        for cx in range(nx):
            for ch in range(nh):
                for cy in range(ny):
                    for ck in range(nk):
                        src = (((cx * nh + ch) * ny + cy) * nk + ck) * corners
                        dst = (((ck * nx + cx) * ny + cy) * nh + ch) * corners
                        Kt[dst : dst + corners, :] = turned[src : src + corners, :]
        K[...] = Kt[...].T.astype(BF16)

    def build_corner(j, right):
        block = jnp.concatenate(
            [mm(right, bwd[j]), -coupling[j, :, :face].astype(F32)],
            axis=0,
        )
        above = 2 * corners * j
        below = LANES - above - 2 * corners
        parts = [block]
        if above:
            parts = [jnp.zeros((above, face), F32)] + parts
        if below:
            parts = parts + [jnp.zeros((below, face), F32)]
        block = jnp.concatenate(parts, axis=0)
        D[j] = block.astype(BF16)
        Dt[j] = block.T.astype(BF16)

    right_copies = [
        copy(i, SEM_RIGHT, right_send.at[i], right_recv.at[i], at(sub=lax.rem(s + 1, n_sub)))
        for i in range(SOLVES)
    ]
    face_copies = [
        copy(i, SEM_FACE, face_send.at[i], face_recv.at[i], at(sub=lax.rem(s + n_sub - 1, n_sub)))
        for i in range(SOLVES)
    ]

    def first_local(slot):
        right = mm(S[0, face:, :], f[0]).astype(BF16)
        left[0] = mm(S[0, :face, :], f[0])
        base[1] = mm(fwd[1], right)

    def second_local(slot):
        right_send[slot] = mm(S[1, face:, :], f[1]).astype(BF16)

        @pl.when(s < n_sub - 1)
        def _():
            right_copies[slot].start()

        base[1] = base[1] - mm(S[1, :face, :], f[1])

    def gather_start(slot, copies):
        for c in copies:
            c.wait_recv()
        halves = []
        for ch in range(nh):
            summed = R[slot, ch * n_sub].astype(F32)
            for a in range(1, n_sub):
                summed = summed + R[slot, ch * n_sub + a].astype(F32)
            halves.append(summed)
        G[slot, k * nx * ny + xy] = jnp.concatenate(halves, axis=0).astype(BF16)
        piece = G.at[slot, k * nx * ny + xy]
        return {
            d: start(copy(slot, SEM_XY + d[0] * ny + d[1], piece, piece, xy_at(*d)))
            for d in xy_steps
        }

    def gather_end(slot, copies):
        passed = []
        for dx in sorted(range(nx), key=lambda d: min(d, nx - d)):
            for dy in range(ny):
                if (dx, dy) in copies:
                    copies[dx, dy].wait_recv()
            first = k * nx * ny + lax.rem(x - dx + nx, nx) * ny
            block = G.at[slot, pl.ds(first, ny)]
            passed.append(
                start(copy(slot, SEM_K + dx, block, block, at(ck=lax.rem(k + 1, nk))))
            )
        for c in passed:
            c.wait_recv()
        gathered = G[slot]
        gathered = gathered.reshape(gathered.shape[0] * gathered.shape[1], LANES)
        V[slot, s] = mm(K[...], gathered)[:column].astype(BF16)
        piece = V.at[slot, s]
        return [
            start(copy(slot, SEM_E + ds, piece, piece, at(sub=lax.rem(s + ds, n_sub))))
            for ds in range(1, n_sub)
        ]

    def base_of_first(slot):
        @pl.when(s > 0)
        def _():
            right_copies[slot].wait_recv()
            base[0] = mm(fwd[0], right_recv[slot]) - left[0]

        @pl.when(s == 0)
        def _():
            base[0] = jnp.zeros_like(left[0])

    def image(slot, copies):
        for c in copies:
            c.wait_recv()
        summed = V[slot, 0].astype(F32)
        for a in range(1, n_sub):
            summed = summed + V[slot, a].astype(F32)
        cv[0:column, :] = summed.astype(BF16)
        picked = mm(E[...], cv[...]).astype(BF16)
        for j in range(2):
            W[slot, j] = base[j] + mm(Dt[j], picked)

    def turn(slot):
        for j in range(2):
            Wn[slot, j] = W[slot, j].T

    build_permutations(1)
    for load in loads:
        load.wait()
    second = mm(S[1, face:, :], f[1]).astype(BF16)
    right_send[0] = second

    @pl.when(s < n_sub - 1)
    def _():
        right_copies[0].start()

    copies_c = gather_start(0, copies_b)
    first_local(0)
    base[1] = base[1] - mm(S[1, :face, :], f[1])
    build_coarse()
    cv[...] = jnp.zeros_like(cv)
    copies_e = gather_end(0, copies_c)
    build_permutations(0)
    build_corner(1, coupling[0, :, face:])

    @pl.when(s > 0)
    def _():
        coupling_copy.wait_recv()
        entry_copy.wait_recv()
        build_corner(0, prev_coupling[...])
        entry[0:corners, :] = prev_entry[...].astype(F32)

    @pl.when(s == 0)
    def _():
        D[0] = jnp.zeros_like(D[0])
        Dt[0] = jnp.zeros_like(Dt[0])

    E[...] = entry[...].astype(BF16)
    turned = entry[...].T.astype(BF16)
    Et[:, 0:LANES] = turned
    Et[:, LANES:] = turned
    base_of_first(0)
    image(0, copies_e)

    def product(a, b):
        summed = jnp.sum(a[0] * b[0], axis=0, keepdims=True)
        return summed + jnp.sum(a[1] * b[1], axis=0, keepdims=True)

    for slot in range(1, SOLVES):
        v = [W[slot - 1, j].astype(BF16) for j in range(2)]
        terms = mm(D[0], v[0]) + mm(D[1], v[1])
        copies_b = send_column(slot, mm(Et[...], jnp.concatenate(upper_lower(terms), axis=0)))
        face_send[slot] = mm(bwd[0], v[0]).astype(BF16)

        @pl.when(s > 0)
        def _():
            face_copies[slot].start()

        f[0, face:, :] = mm(bwd[1], v[1]).astype(BF16)
        for j in range(2):
            f[j, :face, :] = -v[j]
        first_local(slot)
        copies_c = gather_start(slot, copies_b)

        @pl.when(s < n_sub - 1)
        def _():
            face_copies[slot].wait_recv()
            f[1, face:, :] = face_recv[slot]

        @pl.when(s == n_sub - 1)
        def _():
            f[1, face:, :] = jnp.zeros((face, LANES), BF16)

        second_local(slot)
        copies_e = gather_end(slot, copies_c)
        turn(slot - 1)
        if slot == 1:
            dots[...] = jnp.zeros_like(dots)
            dots[0:1, :] = product(W[0], W[0])
        else:
            dots[1:2, :] = product(W[0], W[1])
            dots[2:3, :] = product(W[1], W[1])
        base_of_first(slot)
        image(slot, copies_e)

    dots[3:4, :] = product(W[0], W[2])
    dots[4:5, :] = product(W[1], W[2])

    here = z * nk + k
    copies = [
        start(
            remote(
                dots,
                dots_a.at[here],
                last_send.at[i],
                last_recv.at[i],
                z_at(*d),
            )
        )
        for i, d in enumerate(z_steps)
    ]
    dots_a[here] = dots[...]
    turn(SOLVES - 1)
    for c in copies:
        c.wait_recv()
    dots_b[xy] = jnp.sum(dots_a[...], axis=0)
    copies = [
        start(
            remote(
                dots_b.at[xy],
                dots_b.at[xy],
                last_send.at[len(z_steps) + i],
                last_recv.at[len(z_steps) + i],
                xy_at(*d),
            )
        )
        for i, d in enumerate(xy_steps)
    ]
    for c in copies:
        c.wait_recv()
    sums = jnp.sum(dots_b[...], axis=0)
    rr, rw, ww, rv, wv = (sums[i : i + 1, :] for i in range(5))
    step = rr / rw
    left_over = rr - 2.0 * step * rw + step * step * ww
    gain = 1.0 + left_over / rr
    curvature = gain * gain * rw - gain * step * (rv + ww) + step * step * wv
    second_step = left_over / curvature
    coef[...] = jnp.zeros_like(coef)
    coef[0:1, :] = step + second_step * gain
    coef[1:2, :] = second_step * step
    columns = coef[...].T
    c_one, c_two = columns[:, 0:1], columns[:, 1:2]
    for j in range(2):
        x_out[j] = c_one * Wn[0, j] - c_two * Wn[1, j]
        r_out[j] = Wn[0, j] - c_one * Wn[1, j] + c_two * Wn[2, j]

    for c in sent:
        c.wait_send()

    @pl.when(s < n_sub - 1)
    def _():
        entry_copy.wait_send()
        coupling_copy.wait_send()
        for c in right_copies:
            c.wait_send()

    @pl.when(s > 0)
    def _():
        for c in face_copies[1:]:
            c.wait_send()


def per_device(sizes, schur, coupling, coarse, cases, order, dofs, scene_loads, scene_weights):
    n_sub, nx, nh, ny, nk = sizes
    nz, nxy = nh * n_sub, nx * ny
    corners, face, scenes = dofs.shape[1], order.shape[1], scene_weights.shape[0]
    column = n_sub * corners
    coarse = coarse.reshape(column, coarse.shape[3])
    gathered = coarse.shape[1]
    sems = nz + nxy + nx + n_sub + 4
    last = nz * nk + nxy - 2
    vmem = pl.BlockSpec(memory_space=pltpu.VMEM)
    out = jax.ShapeDtypeStruct((2, scenes, face), F32)
    return pl.pallas_call(
        functools.partial(kernel, sizes),
        out_shape=(out, out),
        in_specs=[pl.BlockSpec(memory_space=pl.ANY)] + [vmem] * 7,
        out_specs=(vmem, vmem),
        scratch_shapes=[
            pltpu.VMEM(schur.shape, BF16),
            pltpu.VMEM((2, face, face), BF16),
            pltpu.VMEM((2, face, face), BF16),
            pltpu.VMEM((LANES, gathered), BF16),
            pltpu.VMEM((gathered, LANES), F32),
            pltpu.VMEM((2, LANES, face), BF16),
            pltpu.VMEM((2, face, LANES), BF16),
            pltpu.VMEM((LANES, LANES), BF16),
            pltpu.VMEM((LANES, 2 * LANES), BF16),
            pltpu.VMEM((LANES, LANES), F32),
            pltpu.VMEM((2, 2 * face, LANES), BF16),
            pltpu.VMEM((2, face, LANES), F32),
            pltpu.VMEM((1, face, LANES), F32),
            pltpu.VMEM((SOLVES, 2, face, LANES), F32),
            pltpu.VMEM((SOLVES, 2, LANES, face), F32),
            pltpu.VMEM((LANES, LANES), BF16),
            pltpu.VMEM((SOLVES, n_sub, corners, LANES), BF16),
            pltpu.VMEM((SOLVES, nz, corners, LANES), BF16),
            pltpu.VMEM((SOLVES, nk * nxy, nh * corners, LANES), BF16),
            pltpu.VMEM((SOLVES, n_sub, column, LANES), BF16),
            pltpu.VMEM((SOLVES, face, LANES), BF16),
            pltpu.VMEM((SOLVES, face, LANES), BF16),
            pltpu.VMEM((SOLVES, face, LANES), BF16),
            pltpu.VMEM((SOLVES, face, LANES), BF16),
            pltpu.VMEM((corners, face), BF16),
            pltpu.VMEM((corners, LANES), BF16),
            pltpu.VMEM((corners, LANES), BF16),
            pltpu.VMEM((8, LANES), F32),
            pltpu.VMEM((nz * nk, 8, LANES), F32),
            pltpu.VMEM((nxy, 8, LANES), F32),
            pltpu.VMEM((LANES, LANES), F32),
            pltpu.SemaphoreType.DMA((2,)),
            pltpu.SemaphoreType.DMA((SOLVES, sems)),
            pltpu.SemaphoreType.DMA((SOLVES, sems)),
            pltpu.SemaphoreType.DMA((last,)),
            pltpu.SemaphoreType.DMA((last,)),
        ],
        compiler_params=pltpu.CompilerParams(collective_id=0, has_side_effects=True),
    )(schur, coupling, coarse, cases, order, dofs, scene_loads, scene_weights)


def solution(mesh):
    if mesh.devices.size == 256:
        sizes = (mesh.shape["sub"], 4, 2, 4, 2)
    else:
        sizes = (mesh.shape["sub"], mesh.shape["coarse"] // 4, 2, 1, 2)
    finer = Mesh(mesh.devices.reshape(sizes), AXES)
    return jax.shard_map(
        functools.partial(per_device, sizes),
        mesh=finer,
        in_specs=(
            P(AXES, None, None),
            P(AXES, None, None),
            P(None, COARSE, None, "sub"),
            P(AXES, None, None),
            P(AXES, None),
            P(AXES, None),
            P(),
            P(),
        ),
        out_specs=(P(AXES, None, None), P(AXES, None, None)),
        check_vma=False,
    )
```

```python
import functools

import jax
import jax.numpy as jnp
from jax import lax
from jax.experimental import pallas as pl
from jax.experimental.pallas import tpu as pltpu
from jax.sharding import Mesh
from jax.sharding import PartitionSpec as P

AXES = ("sub", "coarse_0", "coarse_1", "coarse_2", "coarse_3")
COARSE = AXES[1:]
LANES = 128
SOLVES = 3
VMEM_BYTES = 44 << 20
F32 = jnp.float32
BF16 = jnp.bfloat16


def contract(a, b, da, db):
    return lax.dot_general(a, b, (((da,), (db,)), ((), ())), preferred_element_type=F32)


def mm(a, b):
    return contract(a, b, 1, 0)


def upper_lower(a):
    upper = a.astype(BF16)
    return upper, (a - upper.astype(F32)).astype(BF16)


def kernel(
    sizes,
    schur,
    coupling_in,
    coarse_in,
    cases_in,
    order_in,
    dofs_in,
    scene_loads_in,
    scene_weights_in,
    w_0,
    w_1,
    w_2,
    coef_out,
    S,
    coupling,
    coarse,
    cases,
    order,
    dofs,
    scene_loads,
    scene_weights,
    fwd,
    bwd,
    K,
    Kt,
    Y,
    Yt,
    Z,
    E,
    Et,
    entry,
    f,
    w,
    base,
    Tb,
    H,
    H2,
    cv,
    T,
    R,
    G,
    V,
    A,
    left_send,
    left_recv,
    right_send,
    right_recv,
    own_order,
    own_entry,
    prev_coupling,
    prev_entry,
    next_coupling,
    next_entry,
    next_order,
    dots,
    dots_a,
    dots_b,
    coef,
    W,
    load_sem,
    send_sem,
    recv_sem,
    once_send,
    once_recv,
    last_send,
    last_recv,
):
    n_sub, nx, nh, ny, nk = sizes
    nz = nh * n_sub
    corners = dofs.shape[1]
    face = order.shape[1]
    column = n_sub * corners
    s, x, h, y, k = (lax.axis_index(a) for a in AXES)
    z = h * n_sub + s
    xy = x * ny + y
    group = ((x * nh + h) * ny + y) * nk + k
    has_next = s < n_sub - 1
    has_prev = s > 0

    def at(sub=None, cx=None, ch=None, cy=None, ck=None):
        return (
            s if sub is None else sub,
            x if cx is None else cx,
            h if ch is None else ch,
            y if cy is None else cy,
            k if ck is None else ck,
        )

    def z_at(dz, dk=0):
        other = lax.rem(z + dz, nz)
        return at(sub=lax.rem(other, n_sub), ch=other // n_sub, ck=lax.rem(k + dk, nk))

    def xy_at(dx, dy):
        return at(cx=lax.rem(x + dx, nx), cy=lax.rem(y + dy, ny))

    def sub_at(ds):
        return at(sub=lax.rem(s + ds, n_sub))

    after, before = sub_at(1), sub_at(n_sub - 1)
    z_steps = [(dz, dk) for dk in range(nk) for dz in range(nz) if (dz, dk) != (0, 0)]
    xy_steps = [(dx, dy) for dx in range(nx) for dy in range(ny) if (dx, dy) != (0, 0)]
    xy_steps.sort(key=lambda d: -(min(d[0], nx - d[0]) + min(d[1], ny - d[1])))
    greeted = [z_at(*d) for d in z_steps] + [xy_at(*d) for d in xy_steps]

    barrier = pltpu.get_barrier_semaphore()
    for device in greeted:
        pl.semaphore_signal(barrier, inc=1, device_id=device, device_id_type=pl.DeviceIdType.MESH)
    loads = [
        pltpu.make_async_copy(src, dst, load_sem.at[i])
        for i, (src, dst) in enumerate(
            (
                (scene_loads_in, scene_loads),
                (scene_weights_in, scene_weights),
                (dofs_in, dofs),
                (cases_in, cases),
                (coupling_in, coupling),
                (order_in, order),
                (schur.at[1], S.at[1]),
                (schur.at[0], S.at[0]),
                (coarse_in, coarse),
            )
        )
    ]
    for load in loads:
        load.start()
    early, load_order, load_second, load_first, load_coarse = loads[:5], *loads[5:]

    sent = []

    def remote(src, dst, send, recv, device):
        return pltpu.make_async_remote_copy(
            src_ref=src,
            dst_ref=dst,
            send_sem=send,
            recv_sem=recv,
            device_id=device,
            device_id_type=pl.DeviceIdType.MESH,
        )

    SEM_XY = nz
    SEM_K = SEM_XY + nx * ny
    SEM_E = SEM_K + nx
    SEM_LEFT = SEM_E + n_sub
    SEM_RIGHT = SEM_LEFT + 1

    def copy(slot, number, src, dst, device):
        return remote(src, dst, send_sem.at[slot, number], recv_sem.at[slot, number], device)

    def once(number, src, dst, device):
        return remote(src, dst, once_send.at[number], once_recv.at[number], device)

    def start(c):
        c.start()
        sent.append(c)
        return c

    def iota(shape, dim):
        return lax.broadcasted_iota(jnp.int32, shape, dim)

    def stacked(blocks, width):
        rows = sum(b.shape[0] for b in blocks)
        rest = [jnp.zeros((LANES - rows, width), F32)] if rows < LANES else []
        return jnp.concatenate([b.astype(F32) for b in blocks] + rest, axis=0)

    for load in early:
        load.wait()
    case = iota((cases.shape[1], LANES), 0)
    mixing = jnp.where(case == scene_loads[0:1, :], scene_weights[0:1, :], 0.0)
    mixing = mixing + jnp.where(case == scene_loads[1:2, :], scene_weights[1:2, :], 0.0)
    mix_0 = mixing.astype(BF16)
    mix_1, mix_2 = upper_lower(mixing - mix_0.astype(F32))
    mix = jnp.concatenate([mix_0, mix_1, mix_2], axis=0)
    for j in range(2):
        thrice = jnp.concatenate([cases[j]] * 3, axis=0)
        f[j] = contract(thrice, mix, 0, 0).astype(BF16)

    eye = (iota((corners, corners), 0) == iota((corners, corners), 1)).astype(BF16)
    entry[...] = jnp.zeros_like(entry)
    total = jnp.zeros((LANES, LANES), F32)
    stride = nx * nh * ny * nk * corners
    for j in range(2):
        shifted = dofs[j : j + 1, :] - group * corners
        local = shifted
        for a in range(1, n_sub):
            local = local - jnp.where(shifted >= a * stride, stride - corners, 0)
        table = (iota((LANES, corners), 0) == local).astype(F32).astype(BF16)
        rows = contract(eye, table, 1, 1)
        entry[(j + 1) * corners : (j + 2) * corners, :] = rows
        own_entry[j] = rows.astype(BF16)
        for part in upper_lower(mm(coupling[j], f[j])):
            total = total + mm(table, part)
    load_order.wait()
    row_a = order[0:1, :].astype(F32)
    own_order[...] = jnp.broadcast_to(row_a, own_order.shape)

    @pl.when(jnp.logical_not(has_prev))
    def _():
        prev_coupling[...] = jnp.zeros_like(prev_coupling)
        prev_entry[...] = jnp.zeros_like(prev_entry)

    @pl.when(jnp.logical_not(has_next))
    def _():
        next_coupling[...] = jnp.zeros_like(next_coupling)
        next_entry[...] = jnp.zeros_like(next_entry)
        next_order[...] = jnp.zeros_like(next_order)

    pl.semaphore_wait(barrier, len(greeted))

    def send_column(slot, total):
        for a in range(n_sub):
            T[slot, a] = total[a * corners : (a + 1) * corners].astype(BF16)
        copies = [
            start(copy(slot, dz, T.at[slot, lax.rem(z + dz, n_sub)], R.at[slot, z], z_at(dz)))
            for dz in range(1, nz)
        ]
        R[slot, z] = T[slot, s]
        return copies

    copies_b = send_column(0, total)

    to_next = [
        once(0, own_entry.at[1], prev_entry, after),
        once(1, coupling.at[1, :, face:], prev_coupling, after),
    ]
    to_prev = [
        once(2, own_entry.at[0], next_entry, before),
        once(3, own_order, next_order, before),
        once(4, coupling.at[0, :, :face], next_coupling, before),
    ]
    to_next += [
        copy(i, SEM_RIGHT, right_send.at[i], right_recv.at[i], after) for i in range(SOLVES)
    ]
    to_prev += [
        copy(i, SEM_LEFT, left_send.at[i], left_recv.at[i], before) for i in range(SOLVES)
    ]
    init_next, rights = to_next[:2], to_next[2:]
    init_prev, lefts = to_prev[:3], to_prev[3:]

    @pl.when(has_next)
    def _():
        for c in init_next:
            c.start()

    @pl.when(has_prev)
    def _():
        for c in init_prev:
            c.start()

    def build_permutations(j, row):
        for b in range(0, face, LANES):
            ids = (iota((LANES, face), 0) + b).astype(F32)
            bwd[j, b : b + LANES, :] = (ids == row).astype(F32).astype(BF16)
        spread = jnp.broadcast_to(row, (LANES, face)).T
        for b in range(0, face, LANES):
            ids = (iota((face, LANES), 1) + b).astype(F32)
            fwd[j, :, b : b + LANES] = (spread == ids).astype(F32).astype(BF16)

    def build_coarse():
        turned = stacked([coarse[...]], coarse.shape[1]).T
        for cx in range(nx):
            for ch in range(nh):
                for cy in range(ny):
                    for ck in range(nk):
                        src = (((cx * nh + ch) * ny + cy) * nk + ck) * corners
                        dst = (((ck * nx + cx) * ny + cy) * nh + ch) * corners
                        Kt[dst : dst + corners, :] = turned[src : src + corners, :]
        K[...] = Kt[...].T.astype(BF16)

    def local_products(slot):
        right = mm(S[1, face:, :], f[1])
        right_send[slot] = right.astype(BF16)

        @pl.when(has_next)
        def _():
            rights[slot].start()

        if slot == 0:
            load_first.wait()
        left = mm(S[0, :face, :], f[0])
        left_send[slot] = left.astype(BF16)

        @pl.when(has_prev)
        def _():
            lefts[slot].start()

        return left, right

    def local_rest(slot, left, right):
        inner = mm(S[0, face:, :], f[0])
        inner_left = mm(S[1, :face, :], f[1])
        w[0, :face, :] = left.astype(BF16)
        w[0, face:, :] = inner.astype(BF16)
        w[1, :face, :] = inner_left.astype(BF16)
        w[1, face:, :] = right.astype(BF16)
        base[1] = mm(fwd[1], w[0, face:, :]) - inner_left
        base[2] = mm(fwd[2], w[1, face:, :])
        return inner, inner_left

    def column_base():
        terms = mm(Z[0], w[0]) + mm(Z[1], w[1])
        Tb[...] = mm(Et[...], jnp.concatenate(upper_lower(terms), axis=0))

    def gather_start(slot, copies):
        for c in copies:
            c.wait_recv()
        halves = []
        for ch in range(nh):
            summed = R[slot, ch * n_sub].astype(F32)
            for a in range(1, n_sub):
                summed = summed + R[slot, ch * n_sub + a].astype(F32)
            halves.append(summed)
        G[slot, k * nx * ny + xy] = jnp.concatenate(halves, axis=0).astype(BF16)
        piece = G.at[slot, k * nx * ny + xy]
        started = {
            d: start(copy(slot, SEM_XY + d[0] * ny + d[1], piece, piece, xy_at(*d)))
            for d in xy_steps
        }
        if slot < SOLVES - 1:
            return started, []
        own = halves[0]
        for ch in range(1, nh):
            own = jnp.where(h == ch, halves[ch], own)
        A[s] = own.astype(BF16)
        piece = A.at[s]
        return started, [
            start(once(ONCE_A + ds, piece, piece, sub_at(ds))) for ds in range(1, n_sub)
        ]

    ONCE_H = 4
    ONCE_A = ONCE_H + n_sub - 1

    def gather_end(slot, copies):
        passed = []
        for dx in sorted(range(nx), key=lambda d: min(d, nx - d)):
            for dy in range(ny):
                if (dx, dy) in copies:
                    copies[dx, dy].wait_recv()
            first = k * nx * ny + lax.rem(x - dx + nx, nx) * ny
            block = G.at[slot, pl.ds(first, ny)]
            passed.append(
                start(copy(slot, SEM_K + dx, block, block, at(ck=lax.rem(k + 1, nk))))
            )
        for c in passed:
            c.wait_recv()
        gathered = G[slot]
        gathered = gathered.reshape(gathered.shape[0] * gathered.shape[1], LANES)
        return mm(K[...], gathered)

    def share(slot, part):
        V[slot, s] = part[:column].astype(BF16)
        piece = V.at[slot, s]
        return [start(copy(slot, SEM_E + ds, piece, piece, sub_at(ds))) for ds in range(1, n_sub)]

    def outer_bases(slot):
        @pl.when(has_prev)
        def _():
            rights[slot].wait_recv()
            base[0] = mm(fwd[0], right_recv[slot]) - left_send[slot].astype(F32)

        @pl.when(jnp.logical_not(has_prev))
        def _():
            base[0] = jnp.zeros((face, LANES), F32)

        @pl.when(has_next)
        def _():
            lefts[slot].wait_recv()
            base[2] = base[2] - left_recv[slot].astype(F32)

        @pl.when(jnp.logical_not(has_next))
        def _():
            base[2] = jnp.zeros((face, LANES), F32)

    def image(slot, copies):
        for c in copies:
            c.wait_recv()
        summed = V[slot, 0].astype(F32)
        for a in range(1, n_sub):
            summed = summed + V[slot, a].astype(F32)
        cv[0:column, :] = summed.astype(BF16)
        picked = mm(E[...], cv[...]).astype(BF16)
        out = []
        for j in range(2 if slot == SOLVES - 1 else 3):
            whole = base[j] + mm(Yt[j], picked)
            if j < 2:
                W[slot, j] = whole
            out.append(whole.astype(BF16))
        return out

    def turn(slot):
        for j in range(2):
            (w_0, w_1, w_2)[slot][j] = W[slot, j].T

    def product(a, b):
        summed = jnp.sum(a[0].astype(F32) * b[0], axis=0, keepdims=True)
        return summed + jnp.sum(a[1].astype(F32) * b[1], axis=0, keepdims=True)

    load_second.wait()
    left, right = local_products(0)
    build_permutations(1, order[1:2, :].astype(F32))
    copies_c, _ = gather_start(0, copies_b)

    build_permutations(0, row_a)

    @pl.when(has_prev)
    def _():
        for c in init_next:
            c.wait_recv()

    entry[0:corners, :] = prev_entry[...].astype(F32)
    none = jnp.zeros((corners, face), F32)
    keep_prev = jnp.where(has_prev, 1.0, 0.0).astype(F32)
    keep_next = jnp.where(has_next, 1.0, 0.0).astype(F32)
    left_a = coupling[0, :, :face].astype(F32) * keep_prev
    right_a = coupling[0, :, face:]
    left_b = coupling[1, :, :face]
    right_b = coupling[1, :, face:].astype(F32) * keep_next
    moved_a = mm(prev_coupling[...], bwd[0])
    moved_b = mm(right_a, bwd[1])
    blocks_a = stacked([moved_a, -left_a], face)
    blocks_b = stacked([none, moved_b, -left_b.astype(F32)], face)
    for j, blocks in ((0, blocks_a), (1, blocks_b)):
        Y[j] = blocks.astype(BF16)
        Yt[j] = blocks.T.astype(BF16)

    @pl.when(has_next)
    def _():
        for c in init_prev:
            c.wait_recv()

    entry[3 * corners : 4 * corners, :] = next_entry[...].astype(F32)
    E[...] = entry[...].astype(BF16)
    turned = entry[...].T.astype(BF16)
    Et[:, 0:LANES] = turned
    Et[:, LANES:] = turned

    square = contract(Y[0], Y[0], 1, 1) + contract(Y[1], Y[1], 1, 1)
    upper, lower = upper_lower(square)
    square = mm(upper, E[...]) + mm(lower, E[...])
    square = mm(Et[...], jnp.concatenate(upper_lower(square), axis=0))
    H[s] = square[:column]
    piece = H.at[s]
    copies_h = [start(once(ONCE_H + ds, piece, piece, sub_at(ds))) for ds in range(1, n_sub)]

    build_permutations(2, next_order[0:1, :])
    local_rest(0, left, right)
    moved_c = mm(right_b.astype(BF16), bwd[2])
    blocks_c = stacked([none, none, moved_c, -next_coupling[...].astype(F32)], face)
    Yt[2] = blocks_c.T.astype(BF16)
    Z[0, :, :face] = stacked([-moved_a, left_a], face).astype(BF16)
    Z[0, :, face:] = stacked([none, right_a, -mm(left_b, fwd[1])], face).astype(BF16)
    Z[1, :, :face] = stacked([none, -moved_b, left_b], face).astype(BF16)
    Z[1, :, face:] = stacked([none, none, right_b, -mm(next_coupling[...], fwd[2])], face).astype(
        BF16
    )
    column_base()
    load_coarse.wait()
    build_coarse()
    cv[...] = jnp.zeros_like(cv)
    dots[...] = jnp.zeros_like(dots)
    for c in copies_h:
        c.wait_recv()
    square = H[0]
    for a in range(1, n_sub):
        square = square + H[a]
    H2[:, 0:LANES], H2[:, LANES:] = upper_lower(square)

    def send_next(slot, part):
        rounded = part.astype(BF16)
        change = mm(H2[...], jnp.concatenate([rounded, rounded], axis=0))
        return send_column(slot, Tb[0:column, :] + change)

    part = gather_end(0, copies_c)
    copies_b = send_next(1, part)
    copies_e = share(0, part)
    outer_bases(0)

    for slot in range(1, SOLVES):
        v = image(slot - 1, copies_e)
        f[0, :face, :] = -v[0]
        f[0, face:, :] = mm(bwd[1], v[1]).astype(BF16)
        f[1, :face, :] = -v[1]
        f[1, face:, :] = mm(bwd[2], v[2]).astype(BF16)
        copies_c, copies_a = gather_start(slot, copies_b)
        left, right = local_products(slot)
        inner, inner_left = local_rest(slot, left, right)
        if slot < SOLVES - 1:
            column_base()
        else:
            local = jnp.sum(f[0, :face, :].astype(F32) * left, axis=0, keepdims=True)
            local = local + jnp.sum(f[0, face:, :].astype(F32) * inner, axis=0, keepdims=True)
            local = local + jnp.sum(f[1, :face, :].astype(F32) * inner_left, axis=0, keepdims=True)
            local = local + jnp.sum(f[1, face:, :].astype(F32) * right, axis=0, keepdims=True)
            dots[1:2, :] = product(W[0], W[1])
            dots[2:3, :] = product(W[1], W[1])
            for c in copies_a:
                c.wait_recv()
        turn(slot - 1)
        if slot == 1:
            dots[0:1, :] = product(W[0], W[0])
        part = gather_end(slot, copies_c)
        if slot < SOLVES - 1:
            copies_b = send_next(slot + 1, part)
        else:
            for a in range(n_sub):
                block = part[a * corners : (a + 1) * corners]
                local = local + jnp.sum(A[a].astype(F32) * block, axis=0, keepdims=True)
            dots[3:4, :] = local
            here = z * nk + k
            copies = [
                start(remote(dots, dots_a.at[here], last_send.at[i], last_recv.at[i], z_at(*d)))
                for i, d in enumerate(z_steps)
            ]
            dots_a[here] = dots[...]
        copies_e = share(slot, part)
        if slot < SOLVES - 1:
            outer_bases(slot)

    for c in copies:
        c.wait_recv()
    dots_b[xy] = jnp.sum(dots_a[...], axis=0)
    more = len(z_steps)
    copies = [
        start(
            remote(
                dots_b.at[xy],
                dots_b.at[xy],
                last_send.at[more + i],
                last_recv.at[more + i],
                xy_at(*d),
            )
        )
        for i, d in enumerate(xy_steps)
    ]
    outer_bases(SOLVES - 1)
    image(SOLVES - 1, copies_e)
    turn(SOLVES - 1)
    for c in copies:
        c.wait_recv()
    sums = jnp.sum(dots_b[...], axis=0)
    rr, rw, ww, wv = (sums[i : i + 1, :] for i in range(4))
    step = rr / rw
    left_over = rr - 2.0 * step * rw + step * step * ww
    gain = 1.0 + left_over / rr
    curvature = gain * gain * rw - 2.0 * gain * step * ww + step * step * wv
    second_step = left_over / curvature
    coef[...] = jnp.zeros_like(coef)
    coef[0:1, :] = step + second_step * gain
    coef[1:2, :] = second_step * step
    coef_out[...] = coef[...].T

    for c in sent:
        c.wait_send()

    @pl.when(has_next)
    def _():
        for c in to_next:
            c.wait_send()

    @pl.when(has_prev)
    def _():
        for c in to_prev:
            c.wait_send()


def per_device(sizes, schur, coupling, coarse, cases, order, dofs, scene_loads, scene_weights):
    n_sub, nx, nh, ny, nk = sizes
    nz, nxy = nh * n_sub, nx * ny
    corners, face, scenes = dofs.shape[1], order.shape[1], scene_weights.shape[0]
    column = n_sub * corners
    coarse = coarse.reshape(column, coarse.shape[3])
    gathered = coarse.shape[1]
    sems = nz + nxy + nx + n_sub + 4
    last = nz * nk + nxy - 2
    vmem = pl.BlockSpec(memory_space=pltpu.VMEM)
    out = jax.ShapeDtypeStruct((2, scenes, face), F32)
    operands = (schur, coupling, coarse, cases, order, dofs, scene_loads.T, scene_weights.T)
    operands = [pltpu.with_memory_space_constraint(a, pltpu.HBM) for a in operands]
    w_0, w_1, w_2, coef = pl.pallas_call(
        functools.partial(kernel, sizes),
        out_shape=(out, out, out, jax.ShapeDtypeStruct((LANES, LANES), F32)),
        in_specs=[pl.BlockSpec(memory_space=pltpu.HBM)] * 8,
        out_specs=(vmem,) * 4,
        scratch_shapes=[
            pltpu.VMEM(schur.shape, BF16),
            pltpu.VMEM(coupling.shape, BF16),
            pltpu.VMEM(coarse.shape, BF16),
            pltpu.VMEM(cases.shape, BF16),
            pltpu.VMEM(order.shape, jnp.int32),
            pltpu.VMEM(dofs.shape, jnp.int32),
            pltpu.VMEM((2, scenes), jnp.int32),
            pltpu.VMEM((2, scenes), F32),
            pltpu.VMEM((3, face, face), BF16),
            pltpu.VMEM((3, face, face), BF16),
            pltpu.VMEM((LANES, gathered), BF16),
            pltpu.VMEM((gathered, LANES), F32),
            pltpu.VMEM((2, LANES, face), BF16),
            pltpu.VMEM((3, face, LANES), BF16),
            pltpu.VMEM((2, LANES, 2 * face), BF16),
            pltpu.VMEM((LANES, LANES), BF16),
            pltpu.VMEM((LANES, 2 * LANES), BF16),
            pltpu.VMEM((LANES, LANES), F32),
            pltpu.VMEM((2, 2 * face, LANES), BF16),
            pltpu.VMEM((2, 2 * face, LANES), BF16),
            pltpu.VMEM((3, face, LANES), F32),
            pltpu.VMEM((LANES, LANES), F32),
            pltpu.VMEM((n_sub, column, LANES), F32),
            pltpu.VMEM((column, 2 * LANES), BF16),
            pltpu.VMEM((LANES, LANES), BF16),
            pltpu.VMEM((SOLVES, n_sub, corners, LANES), BF16),
            pltpu.VMEM((SOLVES, nz, corners, LANES), BF16),
            pltpu.VMEM((SOLVES, nk * nxy, nh * corners, LANES), BF16),
            pltpu.VMEM((SOLVES, n_sub, column, LANES), BF16),
            pltpu.VMEM((n_sub, corners, LANES), BF16),
            pltpu.VMEM((SOLVES, face, LANES), BF16),
            pltpu.VMEM((SOLVES, face, LANES), BF16),
            pltpu.VMEM((SOLVES, face, LANES), BF16),
            pltpu.VMEM((SOLVES, face, LANES), BF16),
            pltpu.VMEM((8, face), F32),
            pltpu.VMEM((2, corners, LANES), BF16),
            pltpu.VMEM((corners, face), BF16),
            pltpu.VMEM((corners, LANES), BF16),
            pltpu.VMEM((corners, face), BF16),
            pltpu.VMEM((corners, LANES), BF16),
            pltpu.VMEM((8, face), F32),
            pltpu.VMEM((8, LANES), F32),
            pltpu.VMEM((nz * nk, 8, LANES), F32),
            pltpu.VMEM((nxy, 8, LANES), F32),
            pltpu.VMEM((LANES, LANES), F32),
            pltpu.VMEM((SOLVES, 2, face, LANES), F32),
            pltpu.SemaphoreType.DMA((9,)),
            pltpu.SemaphoreType.DMA((SOLVES, sems)),
            pltpu.SemaphoreType.DMA((SOLVES, sems)),
            pltpu.SemaphoreType.DMA((5 + 2 * n_sub,)),
            pltpu.SemaphoreType.DMA((5 + 2 * n_sub,)),
            pltpu.SemaphoreType.DMA((last,)),
            pltpu.SemaphoreType.DMA((last,)),
        ],
        compiler_params=pltpu.CompilerParams(
            collective_id=0, has_side_effects=True, vmem_limit_bytes=VMEM_BYTES
        ),
    )(*operands)
    c_one, c_two = coef[:, 0:1], coef[:, 1:2]
    return c_one * w_0 - c_two * w_1, w_0 - c_one * w_1 + c_two * w_2


def solution(mesh):
    if mesh.devices.size == 256:
        sizes = (mesh.shape["sub"], 4, 2, 4, 2)
    else:
        sizes = (mesh.shape["sub"], mesh.shape["coarse"] // 4, 2, 1, 2)
    finer = Mesh(mesh.devices.reshape(sizes), AXES)
    return jax.shard_map(
        functools.partial(per_device, sizes),
        mesh=finer,
        in_specs=(
            P(AXES, None, None),
            P(AXES, None, None),
            P(None, COARSE, None, "sub"),
            P(AXES, None, None),
            P(AXES, None),
            P(AXES, None),
            P(),
            P(),
        ),
        out_specs=(P(AXES, None, None), P(AXES, None, None)),
        check_vma=False,
    )
```

```python
import functools

import jax
import jax.numpy as jnp
from jax import lax
from jax.experimental import pallas as pl
from jax.experimental.pallas import tpu as pltpu
from jax.sharding import Mesh
from jax.sharding import PartitionSpec as P

AXES = ("sub", "coarse_0", "coarse_1", "coarse_2", "coarse_3")
COARSE = AXES[1:]
LANES = 128
SOLVES = 3
VMEM_BYTES = 44 << 20
F32 = jnp.float32
BF16 = jnp.bfloat16


def contract(a, b, da, db):
    return lax.dot_general(a, b, (((da,), (db,)), ((), ())), preferred_element_type=F32)


def mm(a, b):
    return contract(a, b, 1, 0)


def upper_lower(a):
    upper = a.astype(BF16)
    return upper, (a - upper.astype(F32)).astype(BF16)


def kernel(
    sizes,
    schur,
    coupling_in,
    coarse_in,
    cases_in,
    order_in,
    dofs_in,
    scene_loads_in,
    scene_weights_in,
    w_0,
    w_1,
    w_2,
    coef_out,
    S,
    coupling,
    coarse,
    cases,
    order,
    dofs,
    scene_loads,
    scene_weights,
    fwd,
    bwd,
    K,
    Kt,
    Y,
    Yt,
    Z,
    E,
    Et,
    entry,
    f,
    w,
    base,
    Tb,
    H,
    H2,
    cv,
    T,
    R,
    G,
    V,
    A,
    left_send,
    left_recv,
    right_send,
    right_recv,
    own_order,
    own_entry,
    prev_coupling,
    prev_entry,
    next_coupling,
    next_entry,
    next_order,
    dots,
    dots_a,
    dots_b,
    coef,
    W,
    wb,
    SC,
    load_sem,
    send_sem,
    recv_sem,
    once_send,
    once_recv,
    last_send,
    last_recv,
):
    n_sub, nx, nh, ny, nk = sizes
    nz = nh * n_sub
    corners = dofs.shape[1]
    face = order.shape[1]
    column = n_sub * corners
    s, x, h, y, k = (lax.axis_index(a) for a in AXES)
    z = h * n_sub + s
    xy = x * ny + y
    group = ((x * nh + h) * ny + y) * nk + k
    has_next = s < n_sub - 1
    has_prev = s > 0

    def at(sub=None, cx=None, ch=None, cy=None, ck=None):
        return (
            s if sub is None else sub,
            x if cx is None else cx,
            h if ch is None else ch,
            y if cy is None else cy,
            k if ck is None else ck,
        )

    def z_at(dz, dk=0):
        other = lax.rem(z + dz, nz)
        return at(sub=lax.rem(other, n_sub), ch=other // n_sub, ck=lax.rem(k + dk, nk))

    def xy_at(dx, dy):
        return at(cx=lax.rem(x + dx, nx), cy=lax.rem(y + dy, ny))

    def sub_at(ds):
        return at(sub=lax.rem(s + ds, n_sub))

    after, before = sub_at(1), sub_at(n_sub - 1)
    z_steps = [(dz, dk) for dk in range(nk) for dz in range(nz) if (dz, dk) != (0, 0)]
    xy_steps = [(dx, dy) for dx in range(nx) for dy in range(ny) if (dx, dy) != (0, 0)]
    xy_steps.sort(key=lambda d: -(min(d[0], nx - d[0]) + min(d[1], ny - d[1])))
    greeted = [z_at(*d) for d in z_steps] + [xy_at(*d) for d in xy_steps]

    barrier = pltpu.get_barrier_semaphore()
    for device in greeted:
        pl.semaphore_signal(barrier, inc=1, device_id=device, device_id_type=pl.DeviceIdType.MESH)
    loads = [
        pltpu.make_async_copy(src, dst, load_sem.at[i])
        for i, (src, dst) in enumerate(
            (
                (scene_loads_in, scene_loads),
                (scene_weights_in, scene_weights),
                (dofs_in, dofs),
                (cases_in, cases),
                (coupling_in, coupling),
                (order_in, order),
                (schur.at[1], S.at[1]),
                (schur.at[0], S.at[0]),
                (coarse_in, coarse),
            )
        )
    ]
    for load in loads:
        load.start()
    early, load_order, load_second, load_first, load_coarse = loads[:5], *loads[5:]

    sent = []

    def remote(src, dst, send, recv, device):
        return pltpu.make_async_remote_copy(
            src_ref=src,
            dst_ref=dst,
            send_sem=send,
            recv_sem=recv,
            device_id=device,
            device_id_type=pl.DeviceIdType.MESH,
        )

    SEM_XY = nz
    SEM_K = SEM_XY + nx * ny
    SEM_E = SEM_K + nx
    SEM_LEFT = SEM_E + n_sub
    SEM_RIGHT = SEM_LEFT + 1

    def copy(slot, number, src, dst, device):
        return remote(src, dst, send_sem.at[slot, number], recv_sem.at[slot, number], device)

    def once(number, src, dst, device):
        return remote(src, dst, once_send.at[number], once_recv.at[number], device)

    def start(c):
        c.start()
        sent.append(c)
        return c

    def iota(shape, dim):
        return lax.broadcasted_iota(jnp.int32, shape, dim)

    def stacked(blocks, width):
        rows = sum(b.shape[0] for b in blocks)
        rest = [jnp.zeros((LANES - rows, width), F32)] if rows < LANES else []
        return jnp.concatenate([b.astype(F32) for b in blocks] + rest, axis=0)

    for load in early:
        load.wait()
    case = iota((cases.shape[1], LANES), 0)
    mixing = jnp.where(case == scene_loads[0:1, :], scene_weights[0:1, :], 0.0)
    mixing = mixing + jnp.where(case == scene_loads[1:2, :], scene_weights[1:2, :], 0.0)
    mix_0 = mixing.astype(BF16)
    mix_1, mix_2 = upper_lower(mixing - mix_0.astype(F32))
    mix = jnp.concatenate([mix_0, mix_1, mix_2], axis=0)
    for j in range(2):
        thrice = jnp.concatenate([cases[j]] * 3, axis=0)
        f[j] = contract(thrice, mix, 0, 0).astype(BF16)

    eye = (iota((corners, corners), 0) == iota((corners, corners), 1)).astype(BF16)
    entry[...] = jnp.zeros_like(entry)
    total = jnp.zeros((LANES, LANES), F32)
    stride = nx * nh * ny * nk * corners
    for j in range(2):
        shifted = dofs[j : j + 1, :] - group * corners
        local = shifted
        for a in range(1, n_sub):
            local = local - jnp.where(shifted >= a * stride, stride - corners, 0)
        table = (iota((LANES, corners), 0) == local).astype(F32).astype(BF16)
        rows = contract(eye, table, 1, 1)
        entry[(j + 1) * corners : (j + 2) * corners, :] = rows
        own_entry[j] = rows.astype(BF16)
        for part in upper_lower(mm(coupling[j], f[j])):
            total = total + mm(table, part)
    load_order.wait()
    row_a = order[0:1, :].astype(F32)
    own_order[...] = jnp.broadcast_to(row_a, own_order.shape)

    @pl.when(jnp.logical_not(has_prev))
    def _():
        prev_coupling[...] = jnp.zeros_like(prev_coupling)
        prev_entry[...] = jnp.zeros_like(prev_entry)

    @pl.when(jnp.logical_not(has_next))
    def _():
        next_coupling[...] = jnp.zeros_like(next_coupling)
        next_entry[...] = jnp.zeros_like(next_entry)
        next_order[...] = jnp.zeros_like(next_order)

    pl.semaphore_wait(barrier, len(greeted))

    def send_column(slot, total):
        for a in range(n_sub):
            T[slot, a] = total[a * corners : (a + 1) * corners].astype(BF16)
        copies = [
            start(copy(slot, dz, T.at[slot, lax.rem(z + dz, n_sub)], R.at[slot, z], z_at(dz)))
            for dz in range(1, nz)
        ]
        R[slot, z] = T[slot, s]
        return copies

    copies_b = send_column(0, total)

    to_next = [
        once(0, own_entry.at[1], prev_entry, after),
        once(1, coupling.at[1, :, face:], prev_coupling, after),
    ]
    to_prev = [
        once(2, own_entry.at[0], next_entry, before),
        once(3, own_order, next_order, before),
        once(4, coupling.at[0, :, :face], next_coupling, before),
    ]
    to_next += [
        copy(i, SEM_RIGHT, right_send.at[i], right_recv.at[i], after) for i in range(SOLVES)
    ]
    to_prev += [
        copy(i, SEM_LEFT, left_send.at[i], left_recv.at[i], before) for i in range(SOLVES)
    ]
    init_next, rights = to_next[:2], to_next[2:]
    init_prev, lefts = to_prev[:3], to_prev[3:]

    @pl.when(has_next)
    def _():
        for c in init_next:
            c.start()

    @pl.when(has_prev)
    def _():
        for c in init_prev:
            c.start()

    def build_permutations(j, row):
        for b in range(0, face, LANES):
            ids = (iota((LANES, face), 0) + b).astype(F32)
            bwd[j, b : b + LANES, :] = (ids == row).astype(F32).astype(BF16)
        spread = jnp.broadcast_to(row, (LANES, face)).T
        for b in range(0, face, LANES):
            ids = (iota((face, LANES), 1) + b).astype(F32)
            fwd[j, :, b : b + LANES] = (spread == ids).astype(F32).astype(BF16)

    def build_coarse():
        turned = stacked([coarse[...]], coarse.shape[1]).T
        for cx in range(nx):
            for ch in range(nh):
                for cy in range(ny):
                    for ck in range(nk):
                        src = (((cx * nh + ch) * ny + cy) * nk + ck) * corners
                        dst = (((ck * nx + cx) * ny + cy) * nh + ch) * corners
                        Kt[dst : dst + corners, :] = turned[src : src + corners, :]
        K[...] = Kt[...].T.astype(BF16)

    lower_half, upper_half = slice(0, face), slice(face, 2 * face)
    RIGHT, LEFT, INNER, INNER_LEFT = (
        (1, upper_half),
        (0, lower_half),
        (0, upper_half),
        (1, lower_half),
    )

    def direct(part):
        return mm(S[part], f[part[0]])

    def send_outer(slot, right, left):
        right_send[slot] = right().astype(BF16)

        @pl.when(has_next)
        def _():
            rights[slot].start()

        left_send[slot] = left().astype(BF16)

        @pl.when(has_prev)
        def _():
            lefts[slot].start()

        w[RIGHT] = right_send[slot]
        w[LEFT] = left_send[slot]

    def fill(v):
        f[0, :face, :] = -v[0]
        f[0, face:, :] = mm(bwd[1], v[1]).astype(BF16)
        f[1, :face, :] = -v[1]
        f[1, face:, :] = mm(bwd[2], v[2]).astype(BF16)

    def coarse_response(j):
        for half in (lower_half, upper_half):
            SC[j, half, 0:LANES], SC[j, half, LANES:] = upper_lower(direct((j, half)))

    def column_base():
        terms = mm(Z[0], w[0]) + mm(Z[1], w[1])
        Tb[...] = mm(Et[...], jnp.concatenate(upper_lower(terms), axis=0))

    def gather_start(slot, copies):
        for c in copies:
            c.wait_recv()
        halves = []
        for ch in range(nh):
            summed = R[slot, ch * n_sub].astype(F32)
            for a in range(1, n_sub):
                summed = summed + R[slot, ch * n_sub + a].astype(F32)
            halves.append(summed)
        G[slot, k * nx * ny + xy] = jnp.concatenate(halves, axis=0).astype(BF16)
        piece = G.at[slot, k * nx * ny + xy]
        started = {
            d: start(copy(slot, SEM_XY + d[0] * ny + d[1], piece, piece, xy_at(*d)))
            for d in xy_steps
        }
        if slot < SOLVES - 1:
            return started, []
        own = halves[0]
        for ch in range(1, nh):
            own = jnp.where(h == ch, halves[ch], own)
        A[s] = own.astype(BF16)
        piece = A.at[s]
        return started, [
            start(once(ONCE_A + ds, piece, piece, sub_at(ds))) for ds in range(1, n_sub)
        ]

    ONCE_H = 4
    ONCE_A = ONCE_H + n_sub - 1

    def gather_pass(slot, copies):
        passed = []
        for dx in sorted(range(nx), key=lambda d: min(d, nx - d)):
            for dy in range(ny):
                if (dx, dy) in copies:
                    copies[dx, dy].wait_recv()
            first = k * nx * ny + lax.rem(x - dx + nx, nx) * ny
            block = G.at[slot, pl.ds(first, ny)]
            passed.append(
                start(copy(slot, SEM_K + dx, block, block, at(ck=lax.rem(k + 1, nk))))
            )
        return passed

    def gather_end(slot, passed):
        for c in passed:
            c.wait_recv()
        gathered = G[slot]
        gathered = gathered.reshape(gathered.shape[0] * gathered.shape[1], LANES)
        return mm(K[...], gathered)

    def share(slot, part):
        V[slot, s] = part[:column].astype(BF16)
        piece = V.at[slot, s]
        return [start(copy(slot, SEM_E + ds, piece, piece, sub_at(ds))) for ds in range(1, n_sub)]

    def bases(slot):
        base[1] = mm(fwd[1], w[0, face:, :]) - w[1, :face, :].astype(F32)

        @pl.when(has_prev)
        def _():
            rights[slot].wait_recv()
            base[0] = mm(fwd[0], right_recv[slot]) - left_send[slot].astype(F32)

        @pl.when(jnp.logical_not(has_prev))
        def _():
            base[0] = jnp.zeros((face, LANES), F32)

        @pl.when(has_next)
        def _():
            lefts[slot].wait_recv()
            base[2] = mm(fwd[2], w[1, face:, :]) - left_recv[slot].astype(F32)

        @pl.when(jnp.logical_not(has_next))
        def _():
            base[2] = jnp.zeros((face, LANES), F32)

    def picked_values(slot, copies):
        for c in copies:
            c.wait_recv()
        summed = V[slot, 0].astype(F32)
        for a in range(1, n_sub):
            summed = summed + V[slot, a].astype(F32)
        cv[0:column, :] = summed.astype(BF16)
        return mm(E[...], cv[...]).astype(BF16)

    def image(slot, picked):
        for j in range(2):
            W[slot, j] = base[j] + mm(Yt[j], picked)

    def turn(slot):
        for j in range(2):
            (w_0, w_1, w_2)[slot][j] = W[slot, j].T

    def product(a, b):
        summed = jnp.sum(a[0].astype(F32) * b[0], axis=0, keepdims=True)
        return summed + jnp.sum(a[1].astype(F32) * b[1], axis=0, keepdims=True)

    load_second.wait()

    def second_then_first():
        load_first.wait()
        return direct(LEFT)

    send_outer(0, lambda: direct(RIGHT), second_then_first)
    w[INNER] = direct(INNER).astype(BF16)
    w[INNER_LEFT] = direct(INNER_LEFT).astype(BF16)
    build_permutations(1, order[1:2, :].astype(F32))
    build_permutations(0, row_a)
    load_coarse.wait()
    build_coarse()
    cv[...] = jnp.zeros_like(cv)
    dots[...] = jnp.zeros_like(dots)
    copies_c, _ = gather_start(0, copies_b)

    @pl.when(has_prev)
    def _():
        for c in init_next:
            c.wait_recv()

    entry[0:corners, :] = prev_entry[...].astype(F32)
    none = jnp.zeros((corners, face), F32)
    keep_prev = jnp.where(has_prev, 1.0, 0.0).astype(F32)
    keep_next = jnp.where(has_next, 1.0, 0.0).astype(F32)
    left_a = coupling[0, :, :face].astype(F32) * keep_prev
    right_a = coupling[0, :, face:]
    left_b = coupling[1, :, :face]
    right_b = coupling[1, :, face:].astype(F32) * keep_next
    moved_a = mm(prev_coupling[...], bwd[0])
    moved_b = mm(right_a, bwd[1])
    blocks_a = stacked([moved_a, -left_a], face)
    blocks_b = stacked([none, moved_b, -left_b.astype(F32)], face)
    for j, blocks in ((0, blocks_a), (1, blocks_b)):
        Y[j] = blocks.astype(BF16)
        Yt[j] = blocks.T.astype(BF16)

    @pl.when(has_next)
    def _():
        for c in init_prev:
            c.wait_recv()

    entry[3 * corners : 4 * corners, :] = next_entry[...].astype(F32)
    E[...] = entry[...].astype(BF16)
    turned = entry[...].T.astype(BF16)
    Et[:, 0:LANES] = turned
    Et[:, LANES:] = turned

    square = contract(Y[0], Y[0], 1, 1) + contract(Y[1], Y[1], 1, 1)
    upper, lower = upper_lower(square)
    square = mm(upper, E[...]) + mm(lower, E[...])
    square = mm(Et[...], jnp.concatenate(upper_lower(square), axis=0))
    H[s] = square[:column]
    piece = H.at[s]
    copies_h = [start(once(ONCE_H + ds, piece, piece, sub_at(ds))) for ds in range(1, n_sub)]

    build_permutations(2, next_order[0:1, :])
    moved_c = mm(right_b.astype(BF16), bwd[2])
    blocks_c = stacked([none, none, moved_c, -next_coupling[...].astype(F32)], face)
    Yt[2] = blocks_c.T.astype(BF16)
    Z[0, :, :face] = stacked([-moved_a, left_a], face).astype(BF16)
    Z[0, :, face:] = stacked([none, right_a, -mm(left_b, fwd[1])], face).astype(BF16)
    Z[1, :, :face] = stacked([none, -moved_b, left_b], face).astype(BF16)
    Z[1, :, face:] = stacked([none, none, right_b, -mm(next_coupling[...], fwd[2])], face).astype(
        BF16
    )
    fill((Yt[0], Yt[1], Yt[2]))
    coarse_response(1)
    passed = gather_pass(0, copies_c)
    column_base()
    coarse_response(0)
    for c in copies_h:
        c.wait_recv()
    square = H[0]
    for a in range(1, n_sub):
        square = square + H[a]
    H2[:, 0:LANES], H2[:, LANES:] = upper_lower(square)

    def send_next(slot, part):
        rounded = part.astype(BF16)
        change = mm(H2[...], jnp.concatenate([rounded, rounded], axis=0))
        return send_column(slot, Tb[0:column, :] + change)

    part = gather_end(0, passed)
    copies_b = send_next(1, part)
    copies_e = share(0, part)
    bases(0)

    for slot in range(1, SOLVES):
        fill([base[j].astype(BF16) for j in range(3)])
        for part in (RIGHT, LEFT, INNER):
            wb[part] = direct(part)
        copies_c, copies_a = gather_start(slot, copies_b)
        wb[INNER_LEFT] = direct(INNER_LEFT)
        picked = picked_values(slot - 1, copies_e)
        twice = jnp.concatenate([picked, picked], axis=0)

        def whole(part):
            return wb[part] + mm(SC[part], twice)

        send_outer(slot, lambda: whole(RIGHT), lambda: whole(LEFT))
        w[INNER] = whole(INNER).astype(BF16)
        w[INNER_LEFT] = whole(INNER_LEFT).astype(BF16)
        image(slot - 1, picked)
        if slot < SOLVES - 1:
            passed = gather_pass(slot, copies_c)
            column_base()
            turn(slot - 1)
            dots[0:1, :] = product(W[0], W[0])
        else:
            last = base[2] + mm(Yt[2], picked)
            fill([W[slot - 1, 0].astype(BF16), W[slot - 1, 1].astype(BF16), last.astype(BF16)])
            passed = gather_pass(slot, copies_c)
            local = jnp.zeros((1, LANES), F32)
            for j in range(2):
                terms = f[j].astype(F32) * w[j].astype(F32)
                local = local + jnp.sum(terms, axis=0, keepdims=True)
            dots[1:2, :] = product(W[0], W[1])
            dots[2:3, :] = product(W[1], W[1])
            for c in copies_a:
                c.wait_recv()
        part = gather_end(slot, passed)
        if slot < SOLVES - 1:
            copies_b = send_next(slot + 1, part)
        else:
            for a in range(n_sub):
                block = part[a * corners : (a + 1) * corners]
                local = local + jnp.sum(A[a].astype(F32) * block, axis=0, keepdims=True)
            dots[3:4, :] = local
            here = z * nk + k
            copies = [
                start(remote(dots, dots_a.at[here], last_send.at[i], last_recv.at[i], z_at(*d)))
                for i, d in enumerate(z_steps)
            ]
            dots_a[here] = dots[...]
        copies_e = share(slot, part)
        if slot == SOLVES - 1:
            turn(slot - 1)
        bases(slot)

    for c in copies:
        c.wait_recv()
    dots_b[xy] = jnp.sum(dots_a[...], axis=0)
    more = len(z_steps)
    copies = [
        start(
            remote(
                dots_b.at[xy],
                dots_b.at[xy],
                last_send.at[more + i],
                last_recv.at[more + i],
                xy_at(*d),
            )
        )
        for i, d in enumerate(xy_steps)
    ]
    image(SOLVES - 1, picked_values(SOLVES - 1, copies_e))
    turn(SOLVES - 1)
    for c in copies:
        c.wait_recv()
    sums = jnp.sum(dots_b[...], axis=0)
    rr, rw, ww, wv = (sums[i : i + 1, :] for i in range(4))
    step = rr / rw
    left_over = rr - 2.0 * step * rw + step * step * ww
    gain = 1.0 + left_over / rr
    curvature = gain * gain * rw - 2.0 * gain * step * ww + step * step * wv
    second_step = left_over / curvature
    coef[...] = jnp.zeros_like(coef)
    coef[0:1, :] = step + second_step * gain
    coef[1:2, :] = second_step * step
    coef_out[...] = coef[...].T

    for c in sent:
        c.wait_send()

    @pl.when(has_next)
    def _():
        for c in to_next:
            c.wait_send()

    @pl.when(has_prev)
    def _():
        for c in to_prev:
            c.wait_send()


def per_device(sizes, schur, coupling, coarse, cases, order, dofs, scene_loads, scene_weights):
    n_sub, nx, nh, ny, nk = sizes
    nz, nxy = nh * n_sub, nx * ny
    corners, face, scenes = dofs.shape[1], order.shape[1], scene_weights.shape[0]
    column = n_sub * corners
    coarse = coarse.reshape(column, coarse.shape[3])
    gathered = coarse.shape[1]
    sems = nz + nxy + nx + n_sub + 4
    last = nz * nk + nxy - 2
    vmem = pl.BlockSpec(memory_space=pltpu.VMEM)
    out = jax.ShapeDtypeStruct((2, scenes, face), F32)
    operands = (schur, coupling, coarse, cases, order, dofs, scene_loads.T, scene_weights.T)
    operands = [pltpu.with_memory_space_constraint(a, pltpu.HBM) for a in operands]
    w_0, w_1, w_2, coef = pl.pallas_call(
        functools.partial(kernel, sizes),
        out_shape=(out, out, out, jax.ShapeDtypeStruct((LANES, LANES), F32)),
        in_specs=[pl.BlockSpec(memory_space=pltpu.HBM)] * 8,
        out_specs=(vmem,) * 4,
        scratch_shapes=[
            pltpu.VMEM(schur.shape, BF16),
            pltpu.VMEM(coupling.shape, BF16),
            pltpu.VMEM(coarse.shape, BF16),
            pltpu.VMEM(cases.shape, BF16),
            pltpu.VMEM(order.shape, jnp.int32),
            pltpu.VMEM(dofs.shape, jnp.int32),
            pltpu.VMEM((2, scenes), jnp.int32),
            pltpu.VMEM((2, scenes), F32),
            pltpu.VMEM((3, face, face), BF16),
            pltpu.VMEM((3, face, face), BF16),
            pltpu.VMEM((LANES, gathered), BF16),
            pltpu.VMEM((gathered, LANES), F32),
            pltpu.VMEM((2, LANES, face), BF16),
            pltpu.VMEM((3, face, LANES), BF16),
            pltpu.VMEM((2, LANES, 2 * face), BF16),
            pltpu.VMEM((LANES, LANES), BF16),
            pltpu.VMEM((LANES, 2 * LANES), BF16),
            pltpu.VMEM((LANES, LANES), F32),
            pltpu.VMEM((2, 2 * face, LANES), BF16),
            pltpu.VMEM((2, 2 * face, LANES), BF16),
            pltpu.VMEM((3, face, LANES), F32),
            pltpu.VMEM((LANES, LANES), F32),
            pltpu.VMEM((n_sub, column, LANES), F32),
            pltpu.VMEM((column, 2 * LANES), BF16),
            pltpu.VMEM((LANES, LANES), BF16),
            pltpu.VMEM((SOLVES, n_sub, corners, LANES), BF16),
            pltpu.VMEM((SOLVES, nz, corners, LANES), BF16),
            pltpu.VMEM((SOLVES, nk * nxy, nh * corners, LANES), BF16),
            pltpu.VMEM((SOLVES, n_sub, column, LANES), BF16),
            pltpu.VMEM((n_sub, corners, LANES), BF16),
            pltpu.VMEM((SOLVES, face, LANES), BF16),
            pltpu.VMEM((SOLVES, face, LANES), BF16),
            pltpu.VMEM((SOLVES, face, LANES), BF16),
            pltpu.VMEM((SOLVES, face, LANES), BF16),
            pltpu.VMEM((8, face), F32),
            pltpu.VMEM((2, corners, LANES), BF16),
            pltpu.VMEM((corners, face), BF16),
            pltpu.VMEM((corners, LANES), BF16),
            pltpu.VMEM((corners, face), BF16),
            pltpu.VMEM((corners, LANES), BF16),
            pltpu.VMEM((8, face), F32),
            pltpu.VMEM((8, LANES), F32),
            pltpu.VMEM((nz * nk, 8, LANES), F32),
            pltpu.VMEM((nxy, 8, LANES), F32),
            pltpu.VMEM((LANES, LANES), F32),
            pltpu.VMEM((SOLVES, 2, face, LANES), F32),
            pltpu.VMEM((2, 2 * face, LANES), F32),
            pltpu.VMEM((2, 2 * face, 2 * LANES), BF16),
            pltpu.SemaphoreType.DMA((9,)),
            pltpu.SemaphoreType.DMA((SOLVES, sems)),
            pltpu.SemaphoreType.DMA((SOLVES, sems)),
            pltpu.SemaphoreType.DMA((5 + 2 * n_sub,)),
            pltpu.SemaphoreType.DMA((5 + 2 * n_sub,)),
            pltpu.SemaphoreType.DMA((last,)),
            pltpu.SemaphoreType.DMA((last,)),
        ],
        compiler_params=pltpu.CompilerParams(
            collective_id=0, has_side_effects=True, vmem_limit_bytes=VMEM_BYTES
        ),
    )(*operands)
    c_one, c_two = coef[:, 0:1], coef[:, 1:2]
    return c_one * w_0 - c_two * w_1, w_0 - c_one * w_1 + c_two * w_2


def solution(mesh):
    if mesh.devices.size == 256:
        sizes = (mesh.shape["sub"], 4, 2, 4, 2)
    else:
        sizes = (mesh.shape["sub"], mesh.shape["coarse"] // 4, 2, 1, 2)
    finer = Mesh(mesh.devices.reshape(sizes), AXES)
    return jax.shard_map(
        functools.partial(per_device, sizes),
        mesh=finer,
        in_specs=(
            P(AXES, None, None),
            P(AXES, None, None),
            P(None, COARSE, None, "sub"),
            P(AXES, None, None),
            P(AXES, None),
            P(AXES, None),
            P(),
            P(),
        ),
        out_specs=(P(AXES, None, None), P(AXES, None, None)),
        check_vma=False,
    )
```

```python
import functools

import jax
import jax.numpy as jnp
from jax import lax
from jax.experimental import pallas as pl
from jax.experimental.pallas import tpu as pltpu
from jax.sharding import Mesh
from jax.sharding import PartitionSpec as P

AXES = ("sub", "coarse_0", "coarse_1", "coarse_2", "coarse_3")
COARSE = AXES[1:]
LANES = 128
SOLVES = 3
VMEM_BYTES = 44 << 20
F32 = jnp.float32
BF16 = jnp.bfloat16


def contract(a, b, da, db):
    return lax.dot_general(a, b, (((da,), (db,)), ((), ())), preferred_element_type=F32)


def mm(a, b):
    return contract(a, b, 1, 0)


def upper_lower(a):
    upper = a.astype(BF16)
    return upper, (a - upper.astype(F32)).astype(BF16)


def kernel(
    sizes,
    schur,
    coupling_in,
    coarse_in,
    cases_in,
    order_in,
    dofs_in,
    scene_loads_in,
    scene_weights_in,
    w_0,
    w_1,
    w_2,
    one_out,
    two_out,
    S,
    coupling,
    coarse,
    cases,
    order,
    dofs,
    scene_loads,
    scene_weights,
    fwd,
    bwd,
    K,
    Kt,
    Y,
    Yt,
    Z,
    E,
    Et,
    entry,
    f,
    w,
    base,
    Tb,
    H,
    H2,
    cv,
    T,
    R,
    G,
    V,
    A,
    left_send,
    left_recv,
    right_send,
    right_recv,
    own_order,
    own_entry,
    prev_coupling,
    prev_entry,
    next_coupling,
    next_entry,
    next_order,
    dots,
    dots_a,
    dots_b,
    coef,
    W,
    wb,
    SC,
    load_sem,
    send_sem,
    recv_sem,
    once_send,
    once_recv,
    last_send,
    last_recv,
):
    n_sub, nx, nh, ny, nk = sizes
    nz = nh * n_sub
    corners = dofs.shape[1]
    face = order.shape[1]
    column = n_sub * corners
    s, x, h, y, k = (lax.axis_index(a) for a in AXES)
    z = h * n_sub + s
    xy = x * ny + y
    group = ((x * nh + h) * ny + y) * nk + k
    has_next = s < n_sub - 1
    has_prev = s > 0

    def at(sub=None, cx=None, ch=None, cy=None, ck=None):
        return (
            s if sub is None else sub,
            x if cx is None else cx,
            h if ch is None else ch,
            y if cy is None else cy,
            k if ck is None else ck,
        )

    def z_at(dz, dk=0):
        other = lax.rem(z + dz, nz)
        return at(sub=lax.rem(other, n_sub), ch=other // n_sub, ck=lax.rem(k + dk, nk))

    def xy_at(dx, dy):
        return at(cx=lax.rem(x + dx, nx), cy=lax.rem(y + dy, ny))

    def sub_at(ds):
        return at(sub=lax.rem(s + ds, n_sub))

    after, before = sub_at(1), sub_at(n_sub - 1)
    z_steps = [(dz, dk) for dk in range(nk) for dz in range(nz) if (dz, dk) != (0, 0)]
    xy_steps = [(dx, dy) for dx in range(nx) for dy in range(ny) if (dx, dy) != (0, 0)]
    xy_steps.sort(key=lambda d: -(min(d[0], nx - d[0]) + min(d[1], ny - d[1])))
    greeted = [z_at(*d) for d in z_steps] + [xy_at(*d) for d in xy_steps]

    loads = [
        pltpu.make_async_copy(src, dst, load_sem.at[i])
        for i, (src, dst) in enumerate(
            (
                (scene_loads_in, scene_loads),
                (scene_weights_in, scene_weights),
                (dofs_in, dofs),
                (cases_in, cases),
                (coupling_in, coupling),
                (order_in, order),
                (schur.at[1], S.at[1]),
                (schur.at[0], S.at[0]),
                (coarse_in, coarse),
            )
        )
    ]
    for load in loads:
        load.start()
    barrier = pltpu.get_barrier_semaphore()
    for device in greeted:
        pl.semaphore_signal(barrier, inc=1, device_id=device, device_id_type=pl.DeviceIdType.MESH)
    early, load_order, load_second, load_first, load_coarse = loads[:5], *loads[5:]

    sent = []

    def remote(src, dst, send, recv, device):
        return pltpu.make_async_remote_copy(
            src_ref=src,
            dst_ref=dst,
            send_sem=send,
            recv_sem=recv,
            device_id=device,
            device_id_type=pl.DeviceIdType.MESH,
        )

    SEM_XY = nz
    SEM_K = SEM_XY + nx * ny
    SEM_E = SEM_K + nx
    SEM_LEFT = SEM_E + n_sub
    SEM_RIGHT = SEM_LEFT + 1

    def copy(slot, number, src, dst, device):
        return remote(src, dst, send_sem.at[slot, number], recv_sem.at[slot, number], device)

    def once(number, src, dst, device):
        return remote(src, dst, once_send.at[number], once_recv.at[number], device)

    def start(c):
        c.start()
        sent.append(c)
        return c

    def iota(shape, dim):
        return lax.broadcasted_iota(jnp.int32, shape, dim)

    def stacked(blocks, width):
        rows = sum(b.shape[0] for b in blocks)
        rest = [jnp.zeros((LANES - rows, width), F32)] if rows < LANES else []
        return jnp.concatenate([b.astype(F32) for b in blocks] + rest, axis=0)

    for load in early:
        load.wait()
    case = iota((cases.shape[1], LANES), 0)
    mixing = jnp.where(case == scene_loads[0:1, :], scene_weights[0:1, :], 0.0)
    mixing = mixing + jnp.where(case == scene_loads[1:2, :], scene_weights[1:2, :], 0.0)
    mix_0 = mixing.astype(BF16)
    mix_1, mix_2 = upper_lower(mixing - mix_0.astype(F32))
    mix = jnp.concatenate([mix_0, mix_1, mix_2], axis=0)
    for j in range(2):
        thrice = jnp.concatenate([cases[j]] * 3, axis=0)
        f[j] = contract(thrice, mix, 0, 0).astype(BF16)

    eye = (iota((corners, corners), 0) == iota((corners, corners), 1)).astype(BF16)
    entry[...] = jnp.zeros_like(entry)
    total = jnp.zeros((LANES, LANES), F32)
    stride = nx * nh * ny * nk * corners
    for j in range(2):
        shifted = dofs[j : j + 1, :] - group * corners
        local = shifted
        for a in range(1, n_sub):
            local = local - jnp.where(shifted >= a * stride, stride - corners, 0)
        table = (iota((LANES, corners), 0) == local).astype(F32).astype(BF16)
        rows = contract(eye, table, 1, 1)
        entry[(j + 1) * corners : (j + 2) * corners, :] = rows
        own_entry[j] = rows.astype(BF16)
        for part in upper_lower(mm(coupling[j], f[j])):
            total = total + mm(table, part)
    load_order.wait()
    row_a = order[0:1, :].astype(F32)
    own_order[...] = jnp.broadcast_to(row_a, own_order.shape)

    @pl.when(jnp.logical_not(has_prev))
    def _():
        prev_coupling[...] = jnp.zeros_like(prev_coupling)
        prev_entry[...] = jnp.zeros_like(prev_entry)

    @pl.when(jnp.logical_not(has_next))
    def _():
        next_coupling[...] = jnp.zeros_like(next_coupling)
        next_entry[...] = jnp.zeros_like(next_entry)
        next_order[...] = jnp.zeros_like(next_order)

    pl.semaphore_wait(barrier, len(greeted))

    def send_column(slot, total):
        for a in range(n_sub):
            T[slot, a] = total[a * corners : (a + 1) * corners].astype(BF16)
        copies = [
            start(copy(slot, dz, T.at[slot, lax.rem(z + dz, n_sub)], R.at[slot, z], z_at(dz)))
            for dz in range(1, nz)
        ]
        R[slot, z] = T[slot, s]
        return copies

    copies_b = send_column(0, total)

    to_next = [
        once(0, own_entry.at[1], prev_entry, after),
        once(1, coupling.at[1, :, face:], prev_coupling, after),
    ]
    to_prev = [
        once(2, own_entry.at[0], next_entry, before),
        once(3, own_order, next_order, before),
        once(4, coupling.at[0, :, :face], next_coupling, before),
    ]
    to_next += [
        copy(i, SEM_RIGHT, right_send.at[i], right_recv.at[i], after) for i in range(SOLVES)
    ]
    to_prev += [
        copy(i, SEM_LEFT, left_send.at[i], left_recv.at[i], before) for i in range(SOLVES)
    ]
    init_next, rights = to_next[:2], to_next[2:]
    init_prev, lefts = to_prev[:3], to_prev[3:]

    @pl.when(has_next)
    def _():
        for c in init_next:
            c.start()

    @pl.when(has_prev)
    def _():
        for c in init_prev:
            c.start()

    def build_permutations(j, row):
        for b in range(0, face, LANES):
            ids = (iota((LANES, face), 0) + b).astype(F32)
            bwd[j, b : b + LANES, :] = (ids == row).astype(F32).astype(BF16)
        spread = jnp.broadcast_to(row, (LANES, face)).T
        for b in range(0, face, LANES):
            ids = (iota((face, LANES), 1) + b).astype(F32)
            fwd[j, :, b : b + LANES] = (spread == ids).astype(F32).astype(BF16)

    def build_coarse():
        turned = stacked([coarse[...]], coarse.shape[1]).T
        for cx in range(nx):
            for ch in range(nh):
                for cy in range(ny):
                    for ck in range(nk):
                        src = (((cx * nh + ch) * ny + cy) * nk + ck) * corners
                        dst = (((ck * nx + cx) * ny + cy) * nh + ch) * corners
                        Kt[dst : dst + corners, :] = turned[src : src + corners, :]
        K[...] = Kt[...].T.astype(BF16)

    lower_half, upper_half = slice(0, face), slice(face, 2 * face)
    RIGHT, LEFT, INNER, INNER_LEFT = (
        (1, upper_half),
        (0, lower_half),
        (0, upper_half),
        (1, lower_half),
    )

    def direct(part):
        return mm(S[part], f[part[0]])

    def send_outer(slot, right, left):
        right_send[slot] = right().astype(BF16)

        @pl.when(has_next)
        def _():
            rights[slot].start()

        left_send[slot] = left().astype(BF16)

        @pl.when(has_prev)
        def _():
            lefts[slot].start()

        w[RIGHT] = right_send[slot]
        w[LEFT] = left_send[slot]

    def fill(v):
        f[0, :face, :] = -v[0]
        f[0, face:, :] = mm(bwd[1], v[1]).astype(BF16)
        f[1, :face, :] = -v[1]
        f[1, face:, :] = mm(bwd[2], v[2]).astype(BF16)

    def coarse_response(j):
        for half in (lower_half, upper_half):
            SC[j, half, 0:LANES], SC[j, half, LANES:] = upper_lower(direct((j, half)))

    def column_base():
        terms = mm(Z[0], w[0]) + mm(Z[1], w[1])
        Tb[...] = mm(Et[...], jnp.concatenate(upper_lower(terms), axis=0))

    def gather_start(slot, copies):
        for c in copies:
            c.wait_recv()
        halves = []
        for ch in range(nh):
            summed = R[slot, ch * n_sub].astype(F32)
            for a in range(1, n_sub):
                summed = summed + R[slot, ch * n_sub + a].astype(F32)
            halves.append(summed)
        G[slot, k * nx * ny + xy] = jnp.concatenate(halves, axis=0).astype(BF16)
        piece = G.at[slot, k * nx * ny + xy]
        started = {
            d: start(copy(slot, SEM_XY + d[0] * ny + d[1], piece, piece, xy_at(*d)))
            for d in xy_steps
        }
        if slot < SOLVES - 1:
            return started, []
        own = halves[0]
        for ch in range(1, nh):
            own = jnp.where(h == ch, halves[ch], own)
        A[s] = own.astype(BF16)
        piece = A.at[s]
        return started, [
            start(once(ONCE_A + ds, piece, piece, sub_at(ds))) for ds in range(1, n_sub)
        ]

    ONCE_H = 4
    ONCE_A = ONCE_H + n_sub - 1

    def gather_pass(slot, copies):
        passed = []
        for dx in sorted(range(nx), key=lambda d: min(d, nx - d)):
            for dy in range(ny):
                if (dx, dy) in copies:
                    copies[dx, dy].wait_recv()
            first = k * nx * ny + lax.rem(x - dx + nx, nx) * ny
            block = G.at[slot, pl.ds(first, ny)]
            passed.append(
                start(copy(slot, SEM_K + dx, block, block, at(ck=lax.rem(k + 1, nk))))
            )
        return passed

    def gather_end(slot, passed):
        def half(core):
            rows = G[slot, pl.ds(core * nx * ny, nx * ny)]
            wide = rows.shape[0] * rows.shape[1]
            part = K[:, pl.ds(pl.multiple_of(core * wide, wide), wide)]
            return mm(part, rows.reshape(wide, LANES))

        own = half(k)
        for c in passed:
            c.wait_recv()
        return own + half(1 - k)

    def share(slot, part):
        V[slot, s] = part[:column].astype(BF16)
        piece = V.at[slot, s]
        return [start(copy(slot, SEM_E + ds, piece, piece, sub_at(ds))) for ds in range(1, n_sub)]

    def bases(slot):
        base[1] = mm(fwd[1], w[0, face:, :]) - w[1, :face, :].astype(F32)

        @pl.when(has_prev)
        def _():
            rights[slot].wait_recv()
            base[0] = mm(fwd[0], right_recv[slot]) - left_send[slot].astype(F32)

        @pl.when(jnp.logical_not(has_prev))
        def _():
            base[0] = jnp.zeros((face, LANES), F32)

        @pl.when(has_next)
        def _():
            lefts[slot].wait_recv()
            base[2] = mm(fwd[2], w[1, face:, :]) - left_recv[slot].astype(F32)

        @pl.when(jnp.logical_not(has_next))
        def _():
            base[2] = jnp.zeros((face, LANES), F32)

    def picked_values(slot, copies):
        for c in copies:
            c.wait_recv()
        summed = V[slot, 0].astype(F32)
        for a in range(1, n_sub):
            summed = summed + V[slot, a].astype(F32)
        cv[0:column, :] = summed.astype(BF16)
        return mm(E[...], cv[...]).astype(BF16)

    def image(slot, picked):
        for j in range(2):
            W[slot, j] = base[j] + mm(Yt[j], picked)

    def turn(slot):
        for j in range(2):
            (w_0, w_1, w_2)[slot][j] = W[slot, j].T

    def product(a, b):
        summed = jnp.sum(a[0].astype(F32) * b[0], axis=0, keepdims=True)
        return summed + jnp.sum(a[1].astype(F32) * b[1], axis=0, keepdims=True)

    load_second.wait()

    def second_then_first():
        load_first.wait()
        return direct(LEFT)

    send_outer(0, lambda: direct(RIGHT), second_then_first)
    w[INNER] = direct(INNER).astype(BF16)
    w[INNER_LEFT] = direct(INNER_LEFT).astype(BF16)
    build_permutations(1, order[1:2, :].astype(F32))
    build_permutations(0, row_a)
    load_coarse.wait()
    build_coarse()
    cv[...] = jnp.zeros_like(cv)
    dots[...] = jnp.zeros_like(dots)
    copies_c, _ = gather_start(0, copies_b)

    @pl.when(has_prev)
    def _():
        for c in init_next:
            c.wait_recv()

    entry[0:corners, :] = prev_entry[...].astype(F32)
    none = jnp.zeros((corners, face), F32)
    keep_prev = jnp.where(has_prev, 1.0, 0.0).astype(F32)
    keep_next = jnp.where(has_next, 1.0, 0.0).astype(F32)
    left_a = coupling[0, :, :face].astype(F32) * keep_prev
    right_a = coupling[0, :, face:]
    left_b = coupling[1, :, :face]
    right_b = coupling[1, :, face:].astype(F32) * keep_next
    moved_a = mm(prev_coupling[...], bwd[0])
    moved_b = mm(right_a, bwd[1])
    blocks_a = stacked([moved_a, -left_a], face)
    blocks_b = stacked([none, moved_b, -left_b.astype(F32)], face)
    for j, blocks in ((0, blocks_a), (1, blocks_b)):
        Y[j] = blocks.astype(BF16)
        Yt[j] = blocks.T.astype(BF16)

    @pl.when(has_next)
    def _():
        for c in init_prev:
            c.wait_recv()

    entry[3 * corners : 4 * corners, :] = next_entry[...].astype(F32)
    E[...] = entry[...].astype(BF16)
    turned = entry[...].T.astype(BF16)
    Et[:, 0:LANES] = turned
    Et[:, LANES:] = turned

    square = contract(Y[0], Y[0], 1, 1) + contract(Y[1], Y[1], 1, 1)
    upper, lower = upper_lower(square)
    square = mm(upper, E[...]) + mm(lower, E[...])
    square = mm(Et[...], jnp.concatenate(upper_lower(square), axis=0))
    H[s] = square[:column]
    piece = H.at[s]
    copies_h = [start(once(ONCE_H + ds, piece, piece, sub_at(ds))) for ds in range(1, n_sub)]

    build_permutations(2, next_order[0:1, :])
    moved_c = mm(right_b.astype(BF16), bwd[2])
    blocks_c = stacked([none, none, moved_c, -next_coupling[...].astype(F32)], face)
    Yt[2] = blocks_c.T.astype(BF16)
    Z[0, :, :face] = stacked([-moved_a, left_a], face).astype(BF16)
    Z[0, :, face:] = stacked([none, right_a, -mm(left_b, fwd[1])], face).astype(BF16)
    Z[1, :, :face] = stacked([none, -moved_b, left_b], face).astype(BF16)
    Z[1, :, face:] = stacked([none, none, right_b, -mm(next_coupling[...], fwd[2])], face).astype(
        BF16
    )
    fill((Yt[0], Yt[1], Yt[2]))
    coarse_response(1)
    passed = gather_pass(0, copies_c)
    column_base()
    coarse_response(0)
    for c in copies_h:
        c.wait_recv()
    square = H[0]
    for a in range(1, n_sub):
        square = square + H[a]
    H2[:, 0:LANES], H2[:, LANES:] = upper_lower(square)

    def send_next(slot, part):
        rounded = part.astype(BF16)
        change = mm(H2[...], jnp.concatenate([rounded, rounded], axis=0))
        return send_column(slot, Tb[0:column, :] + change)

    part = gather_end(0, passed)
    copies_b = send_next(1, part)
    copies_e = share(0, part)
    bases(0)

    for slot in range(1, SOLVES):
        fill([base[j].astype(BF16) for j in range(3)])
        for part in (RIGHT, LEFT):
            wb[part] = direct(part)
        copies_c, copies_a = gather_start(slot, copies_b)
        for part in (INNER, INNER_LEFT):
            wb[part] = direct(part)
        picked = picked_values(slot - 1, copies_e)
        twice = jnp.concatenate([picked, picked], axis=0)

        def whole(part):
            return wb[part] + mm(SC[part], twice)

        send_outer(slot, lambda: whole(RIGHT), lambda: whole(LEFT))
        w[INNER] = whole(INNER).astype(BF16)
        w[INNER_LEFT] = whole(INNER_LEFT).astype(BF16)
        image(slot - 1, picked)
        if slot < SOLVES - 1:
            passed = gather_pass(slot, copies_c)
            column_base()
            turn(slot - 1)
            dots[0:1, :] = product(W[0], W[0])
        else:
            last = base[2] + mm(Yt[2], picked)
            fill([W[slot - 1, 0].astype(BF16), W[slot - 1, 1].astype(BF16), last.astype(BF16)])
            passed = gather_pass(slot, copies_c)
            local = jnp.zeros((1, LANES), F32)
            for j in range(2):
                terms = f[j].astype(F32) * w[j].astype(F32)
                local = local + jnp.sum(terms, axis=0, keepdims=True)
            dots[1:2, :] = product(W[0], W[1])
            dots[2:3, :] = product(W[1], W[1])
            for c in copies_a:
                c.wait_recv()
        part = gather_end(slot, passed)
        if slot < SOLVES - 1:
            copies_b = send_next(slot + 1, part)
        else:
            for a in range(n_sub):
                block = part[a * corners : (a + 1) * corners]
                local = local + jnp.sum(A[a].astype(F32) * block, axis=0, keepdims=True)
            dots[3:4, :] = local
            here = z * nk + k
            copies = [
                start(remote(dots, dots_a.at[here], last_send.at[i], last_recv.at[i], z_at(*d)))
                for i, d in enumerate(z_steps)
            ]
            dots_a[here] = dots[...]
        copies_e = share(slot, part)
        if slot == SOLVES - 1:
            turn(slot - 1)
        bases(slot)

    for c in copies:
        c.wait_recv()
    dots_b[xy] = jnp.sum(dots_a[...], axis=0)
    more = len(z_steps)
    copies = [
        start(
            remote(
                dots_b.at[xy],
                dots_b.at[xy],
                last_send.at[more + i],
                last_recv.at[more + i],
                xy_at(*d),
            )
        )
        for i, d in enumerate(xy_steps)
    ]
    image(SOLVES - 1, picked_values(SOLVES - 1, copies_e))
    turn(SOLVES - 1)
    for c in copies:
        c.wait_recv()
    sums = jnp.sum(dots_b[...], axis=0)
    rr, rw, ww, wv = (sums[i : i + 1, :] for i in range(4))
    step = rr / rw
    left_over = rr - 2.0 * step * rw + step * step * ww
    gain = 1.0 + left_over / rr
    curvature = gain * gain * rw - 2.0 * gain * step * ww + step * step * wv
    second_step = left_over / curvature
    coef[...] = jnp.zeros_like(coef)
    coef[0:1, :] = step + second_step * gain
    coef[1:2, :] = second_step * step
    columns = coef[...].T
    one_out[...] = jnp.broadcast_to(columns[:, 0:1], one_out.shape)
    two_out[...] = jnp.broadcast_to(columns[:, 1:2], two_out.shape)

    for c in sent:
        c.wait_send()

    @pl.when(has_next)
    def _():
        for c in to_next:
            c.wait_send()

    @pl.when(has_prev)
    def _():
        for c in to_prev:
            c.wait_send()


def per_device(sizes, schur, coupling, coarse, cases, order, dofs, scene_loads, scene_weights):
    n_sub, nx, nh, ny, nk = sizes
    nz, nxy = nh * n_sub, nx * ny
    corners, face, scenes = dofs.shape[1], order.shape[1], scene_weights.shape[0]
    column = n_sub * corners
    coarse = coarse.reshape(column, coarse.shape[3])
    gathered = coarse.shape[1]
    sems = nz + nxy + nx + n_sub + 4
    last = nz * nk + nxy - 2
    vmem = pl.BlockSpec(memory_space=pltpu.VMEM)
    out = jax.ShapeDtypeStruct((2, scenes, face), F32)
    operands = (schur, coupling, coarse, cases, order, dofs, scene_loads.T, scene_weights.T)
    operands = [pltpu.with_memory_space_constraint(a, pltpu.HBM) for a in operands]
    w_0, w_1, w_2, one, two = pl.pallas_call(
        functools.partial(kernel, sizes),
        out_shape=(out, out, out) + (jax.ShapeDtypeStruct((scenes, face), F32),) * 2,
        in_specs=[pl.BlockSpec(memory_space=pltpu.HBM)] * 8,
        out_specs=(vmem,) * 5,
        scratch_shapes=[
            pltpu.VMEM(schur.shape, BF16),
            pltpu.VMEM(coupling.shape, BF16),
            pltpu.VMEM(coarse.shape, BF16),
            pltpu.VMEM(cases.shape, BF16),
            pltpu.VMEM(order.shape, jnp.int32),
            pltpu.VMEM(dofs.shape, jnp.int32),
            pltpu.VMEM((2, scenes), jnp.int32),
            pltpu.VMEM((2, scenes), F32),
            pltpu.VMEM((3, face, face), BF16),
            pltpu.VMEM((3, face, face), BF16),
            pltpu.VMEM((LANES, gathered), BF16),
            pltpu.VMEM((gathered, LANES), F32),
            pltpu.VMEM((2, LANES, face), BF16),
            pltpu.VMEM((3, face, LANES), BF16),
            pltpu.VMEM((2, LANES, 2 * face), BF16),
            pltpu.VMEM((LANES, LANES), BF16),
            pltpu.VMEM((LANES, 2 * LANES), BF16),
            pltpu.VMEM((LANES, LANES), F32),
            pltpu.VMEM((2, 2 * face, LANES), BF16),
            pltpu.VMEM((2, 2 * face, LANES), BF16),
            pltpu.VMEM((3, face, LANES), F32),
            pltpu.VMEM((LANES, LANES), F32),
            pltpu.VMEM((n_sub, column, LANES), F32),
            pltpu.VMEM((column, 2 * LANES), BF16),
            pltpu.VMEM((LANES, LANES), BF16),
            pltpu.VMEM((SOLVES, n_sub, corners, LANES), BF16),
            pltpu.VMEM((SOLVES, nz, corners, LANES), BF16),
            pltpu.VMEM((SOLVES, nk * nxy, nh * corners, LANES), BF16),
            pltpu.VMEM((SOLVES, n_sub, column, LANES), BF16),
            pltpu.VMEM((n_sub, corners, LANES), BF16),
            pltpu.VMEM((SOLVES, face, LANES), BF16),
            pltpu.VMEM((SOLVES, face, LANES), BF16),
            pltpu.VMEM((SOLVES, face, LANES), BF16),
            pltpu.VMEM((SOLVES, face, LANES), BF16),
            pltpu.VMEM((8, face), F32),
            pltpu.VMEM((2, corners, LANES), BF16),
            pltpu.VMEM((corners, face), BF16),
            pltpu.VMEM((corners, LANES), BF16),
            pltpu.VMEM((corners, face), BF16),
            pltpu.VMEM((corners, LANES), BF16),
            pltpu.VMEM((8, face), F32),
            pltpu.VMEM((8, LANES), F32),
            pltpu.VMEM((nz * nk, 8, LANES), F32),
            pltpu.VMEM((nxy, 8, LANES), F32),
            pltpu.VMEM((LANES, LANES), F32),
            pltpu.VMEM((SOLVES, 2, face, LANES), F32),
            pltpu.VMEM((2, 2 * face, LANES), F32),
            pltpu.VMEM((2, 2 * face, 2 * LANES), BF16),
            pltpu.SemaphoreType.DMA((9,)),
            pltpu.SemaphoreType.DMA((SOLVES, sems)),
            pltpu.SemaphoreType.DMA((SOLVES, sems)),
            pltpu.SemaphoreType.DMA((5 + 2 * n_sub,)),
            pltpu.SemaphoreType.DMA((5 + 2 * n_sub,)),
            pltpu.SemaphoreType.DMA((last,)),
            pltpu.SemaphoreType.DMA((last,)),
        ],
        compiler_params=pltpu.CompilerParams(
            collective_id=0, has_side_effects=True, vmem_limit_bytes=VMEM_BYTES
        ),
    )(*operands)
    return one * w_0 - two * w_1, w_0 - one * w_1 + two * w_2


def solution(mesh):
    if mesh.devices.size == 256:
        sizes = (mesh.shape["sub"], 4, 2, 4, 2)
    else:
        sizes = (mesh.shape["sub"], mesh.shape["coarse"] // 4, 2, 1, 2)
    finer = Mesh(mesh.devices.reshape(sizes), AXES)
    return jax.shard_map(
        functools.partial(per_device, sizes),
        mesh=finer,
        in_specs=(
            P(AXES, None, None),
            P(AXES, None, None),
            P(None, COARSE, None, "sub"),
            P(AXES, None, None),
            P(AXES, None),
            P(AXES, None),
            P(),
            P(),
        ),
        out_specs=(P(AXES, None, None), P(AXES, None, None)),
        check_vma=False,
    )
```
